32 devices in a mesh: vis: 4 (over y, core), row: 4 (over z), col: 2 (over x).
Axes of the slice: x: 2, y: 2, z: 4, core: 2. Of those that a mesh axis runs over, the one named last changes fastest.
Arguments:
- images: bfloat16 [128, 6400], P(('vis', 'row', 'col')), may hold values from -6 to 6
- counts: int32 [4], replicated, may hold values from 1 to 32, 64 in all
- block_order: int32 [4], replicated, may hold values from 0 to 3, each once
- projector_norm_gain: float32 [6400], replicated, may hold values from 0.1 to 1.9
- proj_first: bfloat16 [6400, 4096], P('vis', ('row', 'col')), may hold values from -0.078125 to 0.078125
- proj_bias: float32 [4096], P(('row', 'col')), may hold values from -3 to 3
- proj_second: bfloat16 [4096, 4096], P(('row', 'col'), 'vis'), may hold values from -0.09375 to 0.09375
- gate_weight: bfloat16 [4096, 16384], P('vis', ('row', 'col')), may hold values from -0.09375 to 0.09375
- up_weight: bfloat16 [4096, 16384], P('vis', ('row', 'col')), may hold values from -0.09375 to 0.09375
- down_weight: bfloat16 [16384, 4096], P(('row', 'col'), 'vis'), may hold values from -0.046875 to 0.046875
- cotangent: bfloat16 [64, 4096], P(('row', 'col'), 'vis'), may hold values from -6 to 6
Outputs:
- block_out: bfloat16 [64, 4096], P(('row', 'col'), 'vis')
- image_slot_gradients: float32 [128, 6400], P(('vis', 'row', 'col'))
- first_grad: float32 [6400, 4096], P('vis', ('row', 'col'))
- second_grad: float32 [4096, 4096], P(('row', 'col'), 'vis')
The draws below stay inside these ranges and needn't reach their ends.
Inputs may be any that keep to these rules, and one draw needn't show every extreme that they name: Vision device v's live rows are its first counts[v] slots; the counts sum to 64, and some device's slots are all live. `block_order`: each vision device's index once: the order in which the devices' live rows follow one another among the language rows.
All inputs are finite; a program needn't handle non-finite values.
Results may differ from the reference program's by a relative error of at most 0.034.
Values may be sent and summed in bfloat16 or wider, within the bound.
A program may use at most 64 MiB of HBM per device.

```python
import math
import jax
import jax.numpy as jnp
import numpy as np
from jax import lax

VIT = 6400
PROJ = 4096
D = 4096
FF = 16384
CAP = 32
ROWS = 64
N_VIS = 4


def shard_levels(stream_key, shape, pieces, low, largest):
    level = 1.0
    for dim, shards_of in pieces:
        heights = jax.random.uniform(jax.random.fold_in(jax.random.fold_in(stream_key, 6), dim), (shards_of,), jnp.float32, low / len(pieces), largest / len(pieces))
        level = level * jnp.repeat(jnp.exp(heights), shape[dim] // shards_of).reshape((-1,) + (1,) * (len(shape) - 1 - dim))
    return level


def length_profile(number_of, total, reach, lean):
    loads = [(1 << 20) // math.isqrt(grade ** lean) + 1 for grade in range(2, number_of + 1)]
    spare, given = total - reach - (number_of - 1), [1] * (number_of - 1)
    while spare > 0:
        free = [i for i in range(number_of - 1) if given[i] < reach]
        whole, left = sum([loads[i] for i in free]), spare
        for i in free:
            more = min(reach - given[i], max(1, left * loads[i] // whole), spare)
            given[i] = given[i] + more
            spare = spare - more
    return np.array([reach] + given)


def ragged(stream_key, amount, total, reach, skew):
    if amount == 2:
        one = jax.random.randint(stream_key, (), max(1, total - reach), min(reach, total - 1) + 1)
        return jnp.stack([one, total - one])
    lengths = jnp.asarray(length_profile(amount, total, reach, skew), jnp.int32)
    pairs = (amount - 1) // 2
    source_of, taker = lengths[1:1 + 2 * pairs:2], lengths[2:2 + 2 * pairs:2]
    margin = jnp.minimum(source_of - 1, reach - taker)
    passed = jax.random.randint(jax.random.fold_in(stream_key, 1), (pairs,), 0, 1 << 20) % (margin + 1)
    lengths = lengths.at[1:1 + 2 * pairs:2].set(source_of - passed).at[2:2 + 2 * pairs:2].set(taker + passed)
    return lengths[jax.random.permutation(jax.random.fold_in(stream_key, 2), amount)]


def noise(stream_key, shape, spread, limit, split=(), kind=jnp.bfloat16):
    gain = shard_levels(stream_key, shape, split, -0.22, 0.18) if split else 1.0
    result = jax.random.normal(stream_key, shape, jnp.float32) * spread * gain
    return jnp.minimum(jnp.maximum(result, -limit), limit).astype(kind)


def setup_inputs(seed: int = 0) -> dict:
    key_list = jax.random.split(jax.random.key(seed), 12)
    images = noise(key_list[0], (N_VIS * CAP, VIT), 1.0, 6.0, ((0, 32),))
    counts = ragged(key_list[1], N_VIS, ROWS, CAP, 2).astype(jnp.int32)
    block_order = jax.random.permutation(key_list[2], N_VIS).astype(jnp.int32)
    projector_norm_gain = jnp.clip(1.0 + 0.18 * jax.random.normal(key_list[3], (VIT,), jnp.float32), 0.1, 1.9)
    proj_first = noise(key_list[4], (VIT, PROJ), VIT ** -0.5, 0.078125, ((0, 4), (1, 8)))
    proj_bias = noise(key_list[5], (PROJ,), 0.5, 3.0, ((0, 8),), jnp.float32)
    proj_second = noise(key_list[6], (PROJ, D), PROJ ** -0.5, 0.09375, ((0, 8), (1, 4)))
    gate_weight = noise(key_list[7], (D, FF), D ** -0.5, 0.09375, ((0, 4), (1, 8)))
    up_weight = noise(key_list[8], (D, FF), D ** -0.5, 0.09375, ((0, 4), (1, 8)))
    down_weight = noise(key_list[9], (FF, D), FF ** -0.5, 0.046875, ((0, 8), (1, 4)))
    cotangent = noise(key_list[10], (ROWS, D), 1.0, 6.0, ((0, 8), (1, 4)))
    return dict(images=images, counts=counts, block_order=block_order, projector_norm_gain=projector_norm_gain, proj_first=proj_first, proj_bias=proj_bias, proj_second=proj_second, gate_weight=gate_weight, up_weight=up_weight, down_weight=down_weight, cotangent=cotangent)


def row_tables(counts, block_order, total_rows, per_device, group_size):
    vision = counts.shape[0]
    labels = jnp.arange(vision, dtype=jnp.int32)
    chosen = (block_order[:, None] == labels[None, :]).astype(jnp.int32)
    ordered = lax.optimization_barrier(jnp.sum(chosen * counts[None, :], axis=1)).astype(jnp.int32)
    block_ends = jnp.cumsum(ordered).astype(jnp.int32)
    block_starts = (block_ends - ordered).astype(jnp.int32)
    language = jnp.arange(total_rows, dtype=jnp.int32)
    block_of = lax.optimization_barrier(jnp.sum((block_ends[None, :] <= language[:, None]).astype(jnp.int32), axis=1)).astype(jnp.int32)
    picked = (block_of[:, None] == labels[None, :]).astype(jnp.int32)
    owner = lax.optimization_barrier(jnp.sum(picked * block_order[None, :], axis=1)).astype(jnp.int32)
    offset = (language - lax.optimization_barrier(jnp.sum(picked * block_starts[None, :], axis=1))).astype(jnp.int32)
    stride = vision * per_device
    source = (offset // per_device * stride + owner * per_device + offset % per_device).astype(jnp.int32)
    slots = jnp.arange(stride * group_size, dtype=jnp.int32)
    within = slots % stride
    slot_owner = within // per_device
    slot_offset = (slots // stride * per_device + within % per_device).astype(jnp.int32)
    owner_start = lax.optimization_barrier(jnp.sum(chosen * block_starts[:, None], axis=0)).astype(jnp.int32)
    matched = (slot_owner[:, None] == labels[None, :]).astype(jnp.int32)
    start_of = lax.optimization_barrier(jnp.sum(matched * owner_start[None, :], axis=1)).astype(jnp.int32)
    count_of = lax.optimization_barrier(jnp.sum(matched * counts[None, :], axis=1)).astype(jnp.int32)
    live = slot_offset < count_of
    target = jnp.where(live, start_of + slot_offset, 0).astype(jnp.int32)
    return (source, target, live)

def gelu_parts(pre):
    normal_cdf = 0.5 * (1.0 + jax.scipy.special.erf(pre * 0.7071067811865476))
    density = jnp.exp(-0.5 * pre * pre) * 0.3989422804014327
    return (pre * normal_cdf, normal_cdf + pre * density)

def apply_layer_norm(images, projector_norm_gain):
    values = images.astype(jnp.float32)
    mean_removed = values - lax.optimization_barrier(jnp.mean(values, axis=-1, keepdims=True))
    variance = lax.optimization_barrier(jnp.mean(mean_removed * mean_removed, axis=-1, keepdims=True))
    inverse_scale = lax.rsqrt(variance + 1e-05)
    standardized_input = mean_removed * inverse_scale
    return (standardized_input, inverse_scale, (standardized_input * projector_norm_gain).astype(jnp.bfloat16))

def norm_gradient_pass(gradient_tuple, standardized_input, inverse_scale, projector_norm_gain):
    gain_scaled = gradient_tuple * projector_norm_gain
    return inverse_scale * (gain_scaled - lax.optimization_barrier(jnp.mean(gain_scaled, axis=-1, keepdims=True)) - standardized_input * lax.optimization_barrier(jnp.mean(gain_scaled * standardized_input, axis=-1, keepdims=True)))

def product(left, right):
    return jnp.dot(left, right, preferred_element_type=jnp.float32)

def rounded(value):
    return lax.optimization_barrier(value.astype(jnp.bfloat16)).astype(jnp.float32)

def reference(images, counts, block_order, projector_norm_gain, proj_first, proj_bias, proj_second, gate_weight, up_weight, down_weight, cotangent):
    source, target, live = row_tables(counts, block_order, ROWS, CAP, 1)
    standardized_input, inverse_scale, norm_output = apply_layer_norm(images, projector_norm_gain)
    packed = jnp.take(norm_output, source, axis=0)
    pre = product(packed, proj_first) + proj_bias
    activated, slope = gelu_parts(pre)
    hidden_proj = activated.astype(jnp.bfloat16)
    inputs = product(hidden_proj, proj_second).astype(jnp.bfloat16)
    width = D // N_VIS
    gate_sum = jnp.zeros((ROWS, FF), jnp.float32)
    up_sum = jnp.zeros((ROWS, FF), jnp.float32)
    hidden_grad = jnp.zeros((ROWS, FF), jnp.float32)
    for section in range(N_VIS):
        lower = section * width
        upper = lower + width
        gate_sum = gate_sum + rounded(product(inputs[:, lower:upper], gate_weight[lower:upper]))
        up_sum = up_sum + rounded(product(inputs[:, lower:upper], up_weight[lower:upper]))
        hidden_grad = hidden_grad + rounded(product(cotangent[:, lower:upper], down_weight[:, lower:upper].T))
    gate_sigmoid = jax.nn.sigmoid(gate_sum)
    hidden = (gate_sum * gate_sigmoid * up_sum).astype(jnp.bfloat16)
    block_out = (inputs.astype(jnp.float32) + product(hidden, down_weight)).astype(jnp.bfloat16)
    gate_grad = (hidden_grad * up_sum * gate_sigmoid * (1.0 + gate_sum * (1.0 - gate_sigmoid))).astype(jnp.bfloat16)
    up_grad = (hidden_grad * gate_sum * gate_sigmoid).astype(jnp.bfloat16)
    input_grad = (cotangent.astype(jnp.float32) + product(gate_grad, gate_weight.T) + product(up_grad, up_weight.T)).astype(jnp.bfloat16)
    second_grad = product(hidden_proj.T, input_grad)
    pre_grad = product(input_grad, proj_second.T)
    act_grad = (pre_grad * slope).astype(jnp.bfloat16)
    first_grad = product(packed.T, act_grad)
    normed_grad = product(act_grad, proj_first.T)
    slot_gradient = jnp.where(live[:, None], jnp.take(normed_grad, target, axis=0), jnp.zeros((), jnp.float32))
    image_slot_gradients = norm_gradient_pass(slot_gradient, standardized_input, inverse_scale, projector_norm_gain)
    return (block_out, image_slot_gradients, first_grad, second_grad)
```

```python
import functools

import jax
import jax.numpy as jnp
from jax import lax
from jax.experimental import pallas as pl
from jax.experimental.pallas import tpu as pltpu
from jax.sharding import PartitionSpec as P


def gelu_parts(pre):
    normal_cdf = 0.5 * (1.0 + jax.scipy.special.erf(pre * 0.7071067811865476))
    density = jnp.exp(-0.5 * pre * pre) * 0.3989422804014327
    return (pre * normal_cdf, normal_cdf + pre * density)


def norm_gradient_pass(gradient_tuple, standardized_input, inverse_scale, projector_norm_gain):
    gain_scaled = gradient_tuple * projector_norm_gain
    return inverse_scale * (
        gain_scaled
        - jnp.mean(gain_scaled, axis=-1, keepdims=True)
        - standardized_input * jnp.mean(gain_scaled * standardized_input, axis=-1, keepdims=True)
    )


def feed_grads(hidden_grad, gate_sum, up_sum, gate_sigmoid):
    gate_grad = (
        hidden_grad * up_sum * gate_sigmoid * (1.0 + gate_sum * (1.0 - gate_sigmoid))
    ).astype(jnp.bfloat16)
    up_grad = (hidden_grad * gate_sum * gate_sigmoid).astype(jnp.bfloat16)
    return (gate_grad, up_grad)


MESH = pl.DeviceIdType.MESH
BF = jnp.bfloat16
F32 = jnp.float32
HBM = pl.BlockSpec(memory_space=pltpu.HBM)
VM = pl.BlockSpec(memory_space=pltpu.VMEM)
TILES = 4


def dot_tn(left, right):
    return lax.dot_general(left, right, (((0,), (0,)), ((), ())), preferred_element_type=F32)


def dot_nt(left, right):
    return lax.dot_general(left, right, (((1,), (1,)), ((), ())), preferred_element_type=F32)


def entry_barrier(n, me, coords):
    barrier = pltpu.get_barrier_semaphore()

    def signal(k, carry):
        pl.semaphore_signal(
            barrier, inc=1, device_id=coords(lax.rem(me + k, n)), device_id_type=MESH
        )
        return carry

    lax.fori_loop(1, n, signal, 0)
    return barrier


def spread(src_of, dst, n, me, coords, send_sem, recv_sem, slab=None):
    def body(k, carry):
        p = lax.rem(me + k, n)
        pltpu.make_async_remote_copy(
            src_ref=src_of(p),
            dst_ref=dst.at[me if slab is None else slab],
            send_sem=send_sem,
            recv_sem=recv_sem,
            device_id=coords(p),
            device_id_type=MESH,
        ).start()
        return carry

    lax.fori_loop(1, n, body, 0)


def wait_for(view, sem):
    pltpu.make_async_copy(view, view, sem).wait()


def flat_coords(sizes, p):
    n_vis, _, n_col = sizes
    return (p % n_vis, p // n_vis // n_col, p // n_vis % n_col)


def my_place(sizes):
    n_vis, _, n_col = sizes
    vis, row, col = lax.axis_index("vis"), lax.axis_index("row"), lax.axis_index("col")
    return vis, row, col, (row * n_col + col) * n_vis + vis


def row_places(counts, order, n_vis, per, shape, axis):
    slots = lax.broadcasted_iota(jnp.int32, shape, axis)
    owner = slots // per % n_vis
    offset = slots // (n_vis * per) * per + slots % per
    start_of = jnp.zeros(shape, jnp.int32)
    count_of = jnp.zeros(shape, jnp.int32)
    begin = jnp.int32(0)
    for b in range(n_vis):
        device = order[b]
        live_rows = counts[device]
        start_of = jnp.where(owner == device, begin, start_of)
        count_of = jnp.where(owner == device, live_rows, count_of)
        begin = begin + live_rows
    return jnp.where(offset < count_of, start_of + offset, -1)


def chain_kernel(
    sizes, counts_hbm, order_hbm, images_hbm, gain_hbm, cot_hbm, bias_hbm,
    wf_hbm, ws_hbm, wg_hbm, wu_hbm, wd_hbm,
    block_out, slot_out, first_out, second_out,
    counts, order, images, gain, cot, bias, wf, ws, wg, wu, wd,
    blocks, rows_all, cot_all, upstream, slabs, across, column_sums, returned,
    b_part, b_pair, b_ring, b_all, h_part, h_pair, h_ring, h_all,
    d_part, d_pair, d_ring, d_all, f_part, f_pair, f_ring, f_all,
    c_part, c_recv, c_all, e_part, e_recv, e_all, o_part, o_recv,
    packed_out, act_out, hid_out, ig_out, slope, inputs, acc, hidden, wsem, gather_sems, return_sems, sems,
):
    n_vis, n_row, n_col = sizes
    group = n_row * n_col
    n_dev = n_vis * group
    vis, row, col, me = my_place(sizes)
    pos = row * n_col + col
    core, ring_at, n_ring = lax.rem(vis, 2), vis // 2, n_vis // 2
    per, vf = blocks.shape[1:]
    rows, dl = upstream.shape
    gr, hr = rows // group, rows // 2
    ffl = wg.shape[1]
    tw = ffl // TILES

    def everyone(p):
        return flat_coords(sizes, p)

    def in_ring(p):
        return (2 * p + core, row, col)

    def in_column(p):
        return (lax.rem(p, n_vis), p // n_vis, col)

    def in_group(p):
        return (vis, p // n_col, p % n_col)

    loads = {}
    for i, (name, src, dst) in enumerate(
        (
            ("images", images_hbm, images), ("gain", gain_hbm, gain), ("cot", cot_hbm, cot),
            ("bias", bias_hbm, bias), ("counts", counts_hbm, counts), ("order", order_hbm, order),
            ("wd", wd_hbm, wd), ("wf", wf_hbm, wf), ("ws", ws_hbm, ws), ("wg", wg_hbm, wg), ("wu", wu_hbm, wu),
        )
    ):
        loads[name] = pltpu.make_async_copy(src, dst, wsem.at[i])
        loads[name].start()
    barrier = entry_barrier(n_dev, me, everyone)

    sent = []

    def pair_of_sems(view):
        idx = 2 * len(sent)
        sent.append((view, sems.at[idx]))
        return sems.at[idx], sems.at[idx + 1]

    def start(src_of, dst, n, at, coords):
        view = dst.at[pl.ds(0, n - 1)]
        send_sem, recv_sem = pair_of_sems(view)
        spread(src_of, dst, n, at, coords, send_sem, recv_sem)
        return lambda: wait_for(view, recv_sem)

    def to_partner(src, dst):
        send_sem, recv_sem = pair_of_sems(dst)
        pltpu.make_async_remote_copy(
            src_ref=src, dst_ref=dst, send_sem=send_sem, recv_sem=recv_sem,
            device_id=(2 * ring_at + 1 - core, row, col), device_id_type=MESH,
        ).start()
        return lambda: wait_for(dst, recv_sem)

    def vis_begin(part, pair):
        return to_partner(part.at[1 - core], pair)

    def vis_middle(arrived, part, pair, ring):
        arrived()
        ring[ring_at] = (part[core].astype(F32) + pair[...].astype(F32)).astype(BF)
        return start(lambda p: ring.at[ring_at], ring, n_ring, ring_at, in_ring)

    def vis_finish(arrived, ring, result):
        arrived()
        value = ring[0].astype(F32)
        for i in range(1, n_ring):
            value = value + ring[i].astype(F32)
        result[core] = value.astype(BF)
        return to_partner(result.at[core], result.at[core])

    def fill(part, value, n, chunk):
        for i in range(n):
            part[i] = value[i * chunk:(i + 1) * chunk].astype(BF)

    def total(recv, part, n, at):
        recv[at] = part[at]
        result = recv[0].astype(F32)
        for i in range(1, n):
            result = result + recv[i].astype(F32)
        return result

    def whole(buf, n):
        return jnp.concatenate([buf[i].astype(F32) for i in range(n)], axis=0)

    loads["images"].wait()
    loads["gain"].wait()
    gain_row = gain[...].reshape(1, gain.shape[0])
    values = images[...].astype(F32)
    centred = values - jnp.mean(values, axis=-1, keepdims=True)
    inverse_scale = lax.rsqrt(jnp.mean(centred * centred, axis=-1, keepdims=True) + 1e-05)
    normed = centred * inverse_scale * gain_row
    for i in range(n_vis):
        blocks[i] = normed[:, i * vf:(i + 1) * vf].astype(BF)
    for name in ("cot", "bias", "counts", "order"):
        loads[name].wait()
    pl.semaphore_wait(barrier, n_dev - 1)
    cot_done = start(lambda p: cot, cot_all, group, pos, in_group)
    mates, own = n_row * n_vis, row * n_vis + vis
    row_steps = sorted(range(n_row), key=lambda k: min(k, n_row - k))
    mates_view = rows_all.at[pl.ds(0, mates - 1)]
    send_sem, _ = pair_of_sems(mates_view)
    spread(
        lambda p: blocks.at[lax.rem(p, n_vis)], rows_all, mates, own, in_column,
        send_sem, gather_sems.at[row], slab=me,
    )
    cot_all[pos] = cot[...]
    rows_all[me] = blocks[vis]
    forward_view = rows_all.at[pl.ds(0, mates * (n_col - 1))]
    forward_send, forward_recv = pair_of_sems(forward_view)

    def forward(k):
        r = lax.rem(row + k, n_row)
        wait_for(rows_all.at[pl.ds(0, n_vis - 1 if k == 0 else n_vis)], gather_sems.at[r])
        chunk = rows_all.at[pl.ds((r * n_col + col) * n_vis, n_vis)]
        for j in range(1, n_col):
            pltpu.make_async_remote_copy(
                src_ref=chunk, dst_ref=chunk, send_sem=forward_send, recv_sem=forward_recv,
                device_id=(vis, row, lax.rem(col + j, n_col)), device_id_type=MESH,
            ).start()

    cot_done()
    upstream[...] = whole(cot_all, group).astype(BF)
    loads["wd"].wait()
    steps_left = list(row_steps)
    for t in range(TILES):
        if steps_left:
            forward(steps_left.pop(0))
        cols = slice(t * tw, (t + 1) * tw)
        value = dot_nt(upstream[...], wd[cols, :])
        for i in range(2):
            h_part[i, :, cols] = value[i * hr:(i + 1) * hr].astype(BF)
    for k in steps_left:
        forward(k)
    h_done = vis_begin(h_part, h_pair)
    n_slots = n_dev * per
    place = row_places(counts, order, n_vis, per, (rows, n_slots), 1)
    pick = jnp.where(place == lax.broadcasted_iota(jnp.int32, (rows, n_slots), 0), 1.0, 0.0).astype(BF)

    loads["wf"].wait()
    wait_for(forward_view, forward_recv)
    packed_out[...] = jnp.dot(
        pick, rows_all[...].reshape(n_slots, vf), preferred_element_type=F32
    ).astype(BF)
    fill(b_part, jnp.dot(packed_out[...], wf[...], preferred_element_type=F32), 2, hr)
    b_done = vis_begin(b_part, b_pair)
    b_done = vis_middle(b_done, b_part, b_pair, b_ring)
    h_done = vis_middle(h_done, h_part, h_pair, h_ring)
    b_done = vis_finish(b_done, b_ring, b_all)
    b_done()
    pre = whole(b_all, 2) + bias[...].reshape(1, bias.shape[0])
    activated, slope_value = gelu_parts(pre)
    slope[...] = slope_value
    hid_out[...] = activated.astype(BF)

    loads["ws"].wait()
    fill(c_part, jnp.dot(hid_out[...], ws[...], preferred_element_type=F32), group, gr)
    c_done = start(lambda p: c_part.at[p], c_recv, group, pos, in_group)
    h_done = vis_finish(h_done, h_ring, h_all)
    c_done()
    c_all[pos] = total(c_recv, c_part, group, pos).astype(BF)
    c_done = start(lambda p: c_all.at[pos], c_all, group, pos, in_group)
    loads["wg"].wait()
    loads["wu"].wait()
    h_done()
    c_done()
    inputs[...] = whole(c_all, group).astype(BF)

    d_done = [None] * TILES
    for t in range(TILES):
        cols = slice(t * tw, (t + 1) * tw)
        for half, weight in enumerate((wg, wu)):
            value = jnp.dot(inputs[...], weight[:, cols], preferred_element_type=F32)
            for i in range(2):
                d_part[t, i, :, half * tw:(half + 1) * tw] = value[i * hr:(i + 1) * hr].astype(BF)
        d_done[t] = vis_begin(d_part.at[t], d_pair.at[t])
        if t > 0:
            d_done[t - 1] = vis_middle(d_done[t - 1], d_part.at[t - 1], d_pair.at[t - 1], d_ring.at[t - 1])
    d_done[-1] = vis_middle(d_done[-1], d_part.at[TILES - 1], d_pair.at[TILES - 1], d_ring.at[TILES - 1])
    d_done[0] = vis_finish(d_done[0], d_ring.at[0], d_all.at[0])
    for t in range(TILES):
        if t + 1 < TILES:
            d_done[t + 1] = vis_finish(d_done[t + 1], d_ring.at[t + 1], d_all.at[t + 1])
        d_done[t]()
        cols = slice(t * tw, (t + 1) * tw)
        both = whole(d_all.at[t], 2)
        gate_sum, up_sum = both[:, :tw], both[:, tw:]
        hidden_grad = jnp.concatenate([h_all[i, :, cols].astype(F32) for i in range(2)], axis=0)
        gate_sigmoid = jax.nn.sigmoid(gate_sum)
        hidden[:, cols] = (gate_sum * gate_sigmoid * up_sum).astype(BF)
        gate_grad, up_grad = feed_grads(hidden_grad, gate_sum, up_sum, gate_sigmoid)
        value = dot_nt(gate_grad, wg[:, cols]) + dot_nt(up_grad, wu[:, cols])
        if t == 0:
            acc[...] = value
        else:
            acc[...] += value
    fill(e_part, acc[...], group, gr)
    e_done = start(lambda p: e_part.at[p], e_recv, group, pos, in_group)

    fill(o_part, jnp.dot(hidden[...], wd[...], preferred_element_type=F32), group, gr)
    e_done()
    e_all[pos] = (total(e_recv, e_part, group, pos) + cot[...].astype(F32)).astype(BF)
    e_done = start(lambda p: e_all.at[pos], e_all, group, pos, in_group)
    o_done = start(lambda p: o_part.at[p], o_recv, group, pos, in_group)
    place = row_places(counts, order, n_vis, per, (n_slots, rows), 0)
    put = jnp.where(place == lax.broadcasted_iota(jnp.int32, (n_slots, rows), 1), 1.0, 0.0).astype(BF)
    e_done()
    ig_out[...] = whole(e_all, group).astype(BF)
    fill(f_part, dot_nt(ig_out[...], ws[...]), 2, hr)
    f_done = vis_begin(f_part, f_pair)
    half = hid_out.shape[1] // 2
    second_out[:half] = dot_tn(hid_out[:, :half], ig_out[...])
    f_done = vis_middle(f_done, f_part, f_pair, f_ring)
    second_out[half:] = dot_tn(hid_out[:, half:], ig_out[...])
    o_done()
    block_out[...] = (c_all[pos].astype(F32) + total(o_recv, o_part, group, pos)).astype(BF)
    f_done = vis_finish(f_done, f_ring, f_all)
    f_done()
    act_out[...] = (whole(f_all, 2) * slope[...]).astype(BF)

    slot_act = jnp.dot(put, act_out[...], preferred_element_type=F32).astype(BF)
    slabs[...] = dot_nt(slot_act, wf[...]).astype(BF).reshape(n_dev, per, vf)
    across_send, _ = pair_of_sems(slabs.at[pl.ds(0, mates * (n_col - 1))])
    returned_view = returned.at[pl.ds(0, mates - 1)]
    back_send, back_recv = pair_of_sems(returned_view)
    back_steps = row_steps[::-1]
    for k in back_steps:
        r = lax.rem(row + k, n_row)
        for j in range(1, n_col):
            other = lax.rem(col + j, n_col)
            pltpu.make_async_remote_copy(
                src_ref=slabs.at[pl.ds((r * n_col + other) * n_vis, n_vis)],
                dst_ref=across.at[r, col], send_sem=across_send, recv_sem=return_sems.at[r],
                device_id=(vis, row, other), device_id_type=MESH,
            ).start()
    first_out[...] = dot_tn(packed_out[...], act_out[...])
    for k in back_steps:
        r = lax.rem(row + k, n_row)
        across[r, col] = slabs[pl.ds((r * n_col + col) * n_vis, n_vis)]
        wait_for(across.at[0, pl.ds(0, n_col - 1)], return_sems.at[r])
        value = across[r, 0].astype(F32)
        for c in range(1, n_col):
            value = value + across[r, c].astype(F32)
        column_sums[r] = value.astype(BF)
        for j in range(1 if k == 0 else 0, n_vis):
            other = lax.rem(vis + j, n_vis)
            pltpu.make_async_remote_copy(
                src_ref=column_sums.at[r, other], dst_ref=returned.at[own],
                send_sem=back_send, recv_sem=back_recv,
                device_id=(other, r, col), device_id_type=MESH,
            ).start()
    returned[own] = column_sums[row, vis]
    wait_for(returned_view, back_recv)
    pieces = []
    for i in range(n_vis):
        value = returned[i].astype(F32)
        for r in range(1, n_row):
            value = value + returned[r * n_vis + i].astype(F32)
        pieces.append(value)
    standardized_input = centred * inverse_scale
    slot_out[...] = norm_gradient_pass(
        jnp.concatenate(pieces, axis=1), standardized_input, inverse_scale, gain_row
    )
    for view, sem in sent:
        wait_for(view, sem)


def store_kernel(*refs):
    sources, targets, sems = refs[:4], refs[4:8], refs[8]
    copies = [pltpu.make_async_copy(a, b, sems.at[i]) for i, (a, b) in enumerate(zip(sources, targets))]
    for copy in copies:
        copy.start()
    for copy in copies:
        copy.wait()


def vis_buffers(n_vis, lead, half_rows, width):
    return [
        pltpu.VMEM(lead + (2, half_rows, width), BF),
        pltpu.VMEM(lead + (half_rows, width), BF),
        pltpu.VMEM(lead + (n_vis // 2, half_rows, width), BF),
        pltpu.VMEM(lead + (2, half_rows, width), BF),
    ]


def on_device(
    sizes,
    images,
    counts,
    block_order,
    projector_norm_gain,
    proj_first,
    proj_bias,
    proj_second,
    gate_weight,
    up_weight,
    down_weight,
    cotangent,
):
    n_vis, n_row, n_col = sizes
    group_size = n_row * n_col
    n_dev = n_vis * group_size
    per_device = images.shape[0]
    local_rows = cotangent.shape[0]
    rows = local_rows * group_size
    vf, units = proj_first.shape
    dl, ffl = gate_weight.shape
    hr = rows // 2
    by_group = pltpu.VMEM((group_size, local_rows, dl), BF)
    by_device = pltpu.VMEM((n_dev, per_device, vf), BF)
    n_sends = 3 * (3 + TILES) + 5 + 5
    results = pl.pallas_call(
        functools.partial(chain_kernel, sizes),
        out_shape=(
            pltpu.VMEM((local_rows, dl), BF),
            pltpu.VMEM(images.shape, F32),
            pltpu.VMEM((vf, units), F32),
            pltpu.VMEM((units, dl), F32),
        ),
        in_specs=[HBM] * 11,
        out_specs=(VM,) * 4,
        scratch_shapes=[
            pltpu.SMEM(counts.shape, jnp.int32),
            pltpu.SMEM(block_order.shape, jnp.int32),
            pltpu.VMEM(images.shape, BF),
            pltpu.VMEM(projector_norm_gain.shape, F32),
            pltpu.VMEM(cotangent.shape, BF),
            pltpu.VMEM(proj_bias.shape, F32),
            pltpu.VMEM(proj_first.shape, BF),
            pltpu.VMEM(proj_second.shape, BF),
            pltpu.VMEM(gate_weight.shape, BF),
            pltpu.VMEM(up_weight.shape, BF),
            pltpu.VMEM(down_weight.shape, BF),
            pltpu.VMEM((n_vis, per_device, vf), BF),
            by_device,
            by_group,
            pltpu.VMEM((rows, dl), BF),
            by_device,
            pltpu.VMEM((n_row, n_col, n_vis, per_device, vf), BF),
            pltpu.VMEM((n_row, n_vis, per_device, vf), BF),
            pltpu.VMEM((n_row * n_vis, per_device, vf), BF),
            *vis_buffers(n_vis, (), hr, units),
            *vis_buffers(n_vis, (), hr, ffl),
            *vis_buffers(n_vis, (TILES,), hr, 2 * ffl // TILES),
            *vis_buffers(n_vis, (), hr, units),
            *[by_group] * 8,
            pltpu.VMEM((rows, vf), BF),
            pltpu.VMEM((rows, units), BF),
            pltpu.VMEM((rows, units), BF),
            pltpu.VMEM((rows, dl), BF),
            pltpu.VMEM((rows, units), F32),
            pltpu.VMEM((rows, dl), BF),
            pltpu.VMEM((rows, dl), F32),
            pltpu.VMEM((rows, ffl), BF),
            pltpu.SemaphoreType.DMA((11,)),
            pltpu.SemaphoreType.DMA((n_row,)),
            pltpu.SemaphoreType.DMA((n_row,)),
            pltpu.SemaphoreType.DMA((2 * n_sends,)),
        ],
        compiler_params=pltpu.CompilerParams(
            collective_id=0, has_side_effects=True, vmem_limit_bytes=40 << 20
        ),
    )(
        *[
            pltpu.with_memory_space_constraint(x, pltpu.HBM)
            for x in (
                counts, block_order, images, projector_norm_gain, cotangent,
                proj_bias, proj_first, proj_second, gate_weight, up_weight, down_weight,
            )
        ]
    )
    return pl.pallas_call(
        store_kernel,
        out_shape=tuple(pltpu.HBM(r.shape, r.dtype) for r in results),
        in_specs=[VM] * 4,
        out_specs=(HBM,) * 4,
        scratch_shapes=[pltpu.SemaphoreType.DMA((4,))],
        compiler_params=pltpu.CompilerParams(vmem_limit_bytes=1 << 20),
    )(*[pltpu.with_memory_space_constraint(r, pltpu.VMEM) for r in results])


def solution(mesh):
    in_specs = (
        P(("vis", "row", "col"), None),
        P(),
        P(),
        P(),
        P("vis", ("row", "col")),
        P(("row", "col")),
        P(("row", "col"), "vis"),
        P("vis", ("row", "col")),
        P("vis", ("row", "col")),
        P(("row", "col"), "vis"),
        P(("row", "col"), "vis"),
    )
    out_specs = (
        P(("row", "col"), "vis"),
        P(("vis", "row", "col"), None),
        P("vis", ("row", "col")),
        P(("row", "col"), "vis"),
    )
    sizes = (mesh.shape["vis"], mesh.shape["row"], mesh.shape["col"])
    return jax.shard_map(
        functools.partial(on_device, sizes), mesh=mesh, in_specs=in_specs, out_specs=out_specs, check_vma=False
    )
```

```python
import functools

import jax
import jax.numpy as jnp
from jax import lax
from jax.experimental import pallas as pl
from jax.experimental.pallas import tpu as pltpu
from jax.sharding import PartitionSpec as P


def gelu_parts(pre):
    normal_cdf = 0.5 * (1.0 + jax.scipy.special.erf(pre * 0.7071067811865476))
    density = jnp.exp(-0.5 * pre * pre) * 0.3989422804014327
    return (pre * normal_cdf, normal_cdf + pre * density)


def norm_gradient_pass(gradient_tuple, standardized_input, inverse_scale, projector_norm_gain):
    gain_scaled = gradient_tuple * projector_norm_gain
    return inverse_scale * (
        gain_scaled
        - jnp.mean(gain_scaled, axis=-1, keepdims=True)
        - standardized_input * jnp.mean(gain_scaled * standardized_input, axis=-1, keepdims=True)
    )


def feed_grads(hidden_grad, gate_sum, up_sum, gate_sigmoid):
    gate_grad = (
        hidden_grad * up_sum * gate_sigmoid * (1.0 + gate_sum * (1.0 - gate_sigmoid))
    ).astype(jnp.bfloat16)
    up_grad = (hidden_grad * gate_sum * gate_sigmoid).astype(jnp.bfloat16)
    return (gate_grad, up_grad)


MESH = pl.DeviceIdType.MESH
BF = jnp.bfloat16
F32 = jnp.float32
HBM = pl.BlockSpec(memory_space=pltpu.HBM)
VM = pl.BlockSpec(memory_space=pltpu.VMEM)
TILES = 8


def dot_tn(left, right):
    return lax.dot_general(left, right, (((0,), (0,)), ((), ())), preferred_element_type=F32)


def dot_nt(left, right):
    return lax.dot_general(left, right, (((1,), (1,)), ((), ())), preferred_element_type=F32)


def entry_barrier(devices):
    barrier = pltpu.get_barrier_semaphore()
    for device in devices:
        pl.semaphore_signal(barrier, inc=1, device_id=device, device_id_type=MESH)
    return barrier


def far_first(me, n):
    upper = 2 * me // n
    order = []
    for j in range(n - 1):
        down = n - 1 - j
        down = down - (me - down + n) // n
        up = j + (j - me + n) // n
        order.append(upper * up + (1 - upper) * down)
    return order


def spread(targets, dst, send_sem, recv_sem):
    for src, device in targets:
        pltpu.make_async_remote_copy(
            src_ref=src,
            dst_ref=dst,
            send_sem=send_sem,
            recv_sem=recv_sem,
            device_id=device,
            device_id_type=MESH,
        ).start()


def wait_for(view, sem):
    pltpu.make_async_copy(view, view, sem).wait()


def my_place(sizes):
    n_vis, _, n_col = sizes
    vis, row, col = lax.axis_index("vis"), lax.axis_index("row"), lax.axis_index("col")
    return vis, row, col, (row * n_col + col) * n_vis + vis


def row_places(counts, order, n_vis, per, shape, axis):
    slots = lax.broadcasted_iota(jnp.int32, shape, axis)
    owner = slots // per % n_vis
    offset = slots // (n_vis * per) * per + slots % per
    start_of = jnp.zeros(shape, jnp.int32)
    count_of = jnp.zeros(shape, jnp.int32)
    begin = jnp.int32(0)
    for b in range(n_vis):
        device = order[b]
        live_rows = counts[device]
        start_of = jnp.where(owner == device, begin, start_of)
        count_of = jnp.where(owner == device, live_rows, count_of)
        begin = begin + live_rows
    return jnp.where(offset < count_of, start_of + offset, -1)


def chain_kernel(
    sizes, counts_hbm, order_hbm, images_hbm, gain_hbm, cot_hbm, bias_hbm,
    wf_hbm, ws_hbm, wg_hbm, wu_hbm, wd_hbm,
    block_out, slot_out, first_out, second_out,
    counts, order, images, gain, cot, bias, wf, ws, wg, wu, wd,
    blocks, rows_all, cot_all, upstream, slabs, across, column_sums, returned,
    b_part, b_recv, h_part, h_pair, h_ring, h_all,
    d_part, d_pair, d_ring, d_all, f_part, f_recv,
    c_part, c_recv, c_all, e_part, e_recv, e_all, o_part, o_recv,
    packed_out, act_out, hid_out, ig_out, slope, inputs, acc, hidden, wsem, gather_sems, return_sems, sems,
):
    n_vis, n_row, n_col = sizes
    group = n_row * n_col
    n_dev = n_vis * group
    vis, row, col, me = my_place(sizes)
    pos = row * n_col + col
    core, ring_at, n_ring = lax.rem(vis, 2), vis // 2, n_vis // 2
    per, vf = blocks.shape[1:]
    rows, dl = upstream.shape
    gr, hr = rows // group, rows // 2
    ffl = wg.shape[1]
    tw = ffl // TILES

    def in_ring(p):
        return (2 * p + core, row, col)

    rows_out = far_first(row, n_row)
    other_cols = [lax.rem(col + j, n_col) for j in range(1, n_col)]
    other_vis = [
        (2 * lax.rem(ring_at + k, n_ring) + side) for k in range(1, n_ring) for side in (1 - core, core)
    ] + [2 * ring_at + 1 - core]
    group_order = [(r, c) for r in rows_out for c in (*other_cols, col)] + [(row, c) for c in other_cols]
    mates = [(v, row, col) for v in other_vis] + [(v, r, col) for r in rows_out for v in (*other_vis, vis)]

    loads = {}
    for i, (name, src, dst) in enumerate(
        (
            ("images", images_hbm, images), ("gain", gain_hbm, gain), ("cot", cot_hbm, cot),
            ("bias", bias_hbm, bias), ("counts", counts_hbm, counts), ("order", order_hbm, order),
            ("wd", wd_hbm, wd), ("wf", wf_hbm, wf), ("ws", ws_hbm, ws), ("wg", wg_hbm, wg), ("wu", wu_hbm, wu),
        )
    ):
        loads[name] = pltpu.make_async_copy(src, dst, wsem.at[i])
        loads[name].start()
    neighbours = mates + [(vis, r, c) for r in (*rows_out, row) for c in other_cols]
    barrier = entry_barrier(neighbours)

    sent = []

    def pair_of_sems(view):
        idx = 2 * len(sent)
        sent.append((view, sems.at[idx]))
        return sems.at[idx], sems.at[idx + 1]

    def start(targets, dst, n, at):
        view = dst.at[pl.ds(0, n - 1)]
        send_sem, recv_sem = pair_of_sems(view)
        spread(targets, dst.at[at], send_sem, recv_sem)
        return lambda: wait_for(view, recv_sem)

    def scatter(part, recv):
        return start([(part.at[r * n_col + c], (vis, r, c)) for r, c in group_order], recv, group, pos)

    def gather(mine, everything):
        return start([(mine, (vis, r, c)) for r, c in group_order], everything, group, pos)

    def share(part, recv):
        return start([(part, (v, row, col)) for v in other_vis], recv, n_vis, vis)

    def to_partner(src, dst):
        send_sem, recv_sem = pair_of_sems(dst)
        pltpu.make_async_remote_copy(
            src_ref=src, dst_ref=dst, send_sem=send_sem, recv_sem=recv_sem,
            device_id=(2 * ring_at + 1 - core, row, col), device_id_type=MESH,
        ).start()
        return lambda: wait_for(dst, recv_sem)

    def vis_begin(part, pair):
        return to_partner(part.at[1 - core], pair)

    def vis_middle(arrived, part, pair, ring):
        arrived()
        ring[ring_at] = (part[core].astype(F32) + pair[...].astype(F32)).astype(BF)
        others = [in_ring(lax.rem(ring_at + k, n_ring)) for k in range(1, n_ring)]
        return start([(ring.at[ring_at], device) for device in others], ring, n_ring, ring_at)

    def vis_finish(arrived, ring, result):
        arrived()
        value = ring[0].astype(F32)
        for i in range(1, n_ring):
            value = value + ring[i].astype(F32)
        result[core] = value.astype(BF)
        return to_partner(result.at[core], result.at[core])

    def fill(part, value, n, chunk):
        for i in range(n):
            part[i] = value[i * chunk:(i + 1) * chunk].astype(BF)

    def total(recv, own, n, at):
        recv[at] = own
        result = recv[0].astype(F32)
        for i in range(1, n):
            result = result + recv[i].astype(F32)
        return result

    def whole(buf, n):
        return jnp.concatenate([buf[i].astype(F32) for i in range(n)], axis=0)

    loads["images"].wait()
    loads["gain"].wait()
    gain_row = gain[...].reshape(1, gain.shape[0])
    values = images[...].astype(F32)
    centred = values - jnp.mean(values, axis=-1, keepdims=True)
    inverse_scale = lax.rsqrt(jnp.mean(centred * centred, axis=-1, keepdims=True) + 1e-05)
    normed = centred * inverse_scale * gain_row
    for i in range(n_vis):
        blocks[i] = normed[:, i * vf:(i + 1) * vf].astype(BF)
    for name in ("cot", "bias", "counts", "order"):
        loads[name].wait()
    pl.semaphore_wait(barrier, len(neighbours))
    own = row * n_vis + vis
    mates_view = rows_all.at[pl.ds(0, len(mates))]
    send_sem, _ = pair_of_sems(mates_view)
    spread([(blocks.at[d[0]], d) for d in mates], rows_all.at[me], send_sem, gather_sems.at[row])
    rows_all[me] = blocks[vis]
    forward_view = rows_all.at[pl.ds(0, n_row * n_vis * (n_col - 1))]
    forward_send, forward_recv = pair_of_sems(forward_view)

    for i, r in enumerate((row, *rows_out[::-1])):
        wait_for(rows_all.at[pl.ds(0, n_vis - 1 if i == 0 else n_vis)], gather_sems.at[r])
        chunk = rows_all.at[pl.ds((r * n_col + col) * n_vis, n_vis)]
        spread([(chunk, (vis, row, c)) for c in other_cols], chunk, forward_send, forward_recv)
    n_slots = n_dev * per
    place = row_places(counts, order, n_vis, per, (rows, n_slots), 1)
    pick = jnp.where(place == lax.broadcasted_iota(jnp.int32, (rows, n_slots), 0), 1.0, 0.0).astype(BF)

    loads["wf"].wait()
    wait_for(forward_view, forward_recv)
    packed_out[...] = jnp.dot(
        pick, rows_all[...].reshape(n_slots, vf), preferred_element_type=F32
    ).astype(BF)
    b_part[...] = jnp.dot(packed_out[...], wf[...], preferred_element_type=F32).astype(BF)
    b_done = share(b_part, b_recv)
    cot_done = gather(cot, cot_all)
    cot_all[pos] = cot[...]
    b_done()
    pre = total(b_recv, b_part[...], n_vis, vis) + bias[...].reshape(1, bias.shape[0])
    activated, slope_value = gelu_parts(pre)
    slope[...] = slope_value
    hid_out[...] = activated.astype(BF)

    loads["ws"].wait()
    fill(c_part, jnp.dot(hid_out[...], ws[...], preferred_element_type=F32), group, gr)
    c_done = scatter(c_part, c_recv)
    cot_done()
    upstream[...] = whole(cot_all, group).astype(BF)
    loads["wd"].wait()
    for t in range(TILES):
        cols = slice(t * tw, (t + 1) * tw)
        value = dot_nt(upstream[...], wd[cols, :])
        for i in range(2):
            h_part[i, :, cols] = value[i * hr:(i + 1) * hr].astype(BF)
    h_done = vis_begin(h_part, h_pair)
    h_done = vis_middle(h_done, h_part, h_pair, h_ring)
    c_done()
    c_all[pos] = total(c_recv, c_part[pos], group, pos).astype(BF)
    c_done = gather(c_all.at[pos], c_all)
    loads["wg"].wait()
    loads["wu"].wait()
    h_done = vis_finish(h_done, h_ring, h_all)
    c_done()
    inputs[...] = whole(c_all, group).astype(BF)

    d_done = [None] * TILES
    for t in range(TILES):
        cols = slice(t * tw, (t + 1) * tw)
        for half, weight in enumerate((wg, wu)):
            value = jnp.dot(inputs[...], weight[:, cols], preferred_element_type=F32)
            for i in range(2):
                d_part[t, i, :, half * tw:(half + 1) * tw] = value[i * hr:(i + 1) * hr].astype(BF)
        d_done[t] = vis_begin(d_part.at[t], d_pair.at[t])
        if t > 0:
            d_done[t - 1] = vis_middle(d_done[t - 1], d_part.at[t - 1], d_pair.at[t - 1], d_ring.at[t - 1])
    d_done[-1] = vis_middle(d_done[-1], d_part.at[TILES - 1], d_pair.at[TILES - 1], d_ring.at[TILES - 1])
    d_done[0] = vis_finish(d_done[0], d_ring.at[0], d_all.at[0])
    for t in range(TILES):
        if t + 1 < TILES:
            d_done[t + 1] = vis_finish(d_done[t + 1], d_ring.at[t + 1], d_all.at[t + 1])
        d_done[t]()
        if t == 0:
            h_done()
        cols = slice(t * tw, (t + 1) * tw)
        both = whole(d_all.at[t], 2)
        gate_sum, up_sum = both[:, :tw], both[:, tw:]
        hidden_grad = jnp.concatenate([h_all[i, :, cols].astype(F32) for i in range(2)], axis=0)
        gate_sigmoid = jax.nn.sigmoid(gate_sum)
        hidden[:, cols] = (gate_sum * gate_sigmoid * up_sum).astype(BF)
        gate_grad, up_grad = feed_grads(hidden_grad, gate_sum, up_sum, gate_sigmoid)
        value = dot_nt(gate_grad, wg[:, cols]) + dot_nt(up_grad, wu[:, cols])
        if t == 0:
            acc[...] = value
        else:
            acc[...] += value
    fill(e_part, acc[...], group, gr)
    e_done = scatter(e_part, e_recv)
    fill(o_part, jnp.dot(hidden[...], wd[...], preferred_element_type=F32), group, gr)
    place = row_places(counts, order, n_vis, per, (n_slots, rows), 0)
    put = jnp.where(place == lax.broadcasted_iota(jnp.int32, (n_slots, rows), 1), 1.0, 0.0).astype(BF)
    e_done()
    e_all[pos] = (total(e_recv, e_part[pos], group, pos) + cot[...].astype(F32)).astype(BF)
    e_done = gather(e_all.at[pos], e_all)
    e_done()
    ig_out[...] = whole(e_all, group).astype(BF)
    f_part[...] = dot_nt(ig_out[...], ws[...]).astype(BF)
    f_done = share(f_part, f_recv)
    o_done = scatter(o_part, o_recv)
    second_out[...] = dot_tn(hid_out[...], ig_out[...])
    f_done()
    act_out[...] = (total(f_recv, f_part[...], n_vis, vis) * slope[...]).astype(BF)

    slot_act = jnp.dot(put, act_out[...], preferred_element_type=F32).astype(BF)
    slabs[...] = dot_nt(slot_act, wf[...]).astype(BF).reshape(n_dev, per, vf)
    across_send, _ = pair_of_sems(slabs.at[pl.ds(0, n_row * n_vis * (n_col - 1))])
    returned_view = returned.at[pl.ds(0, n_row * n_vis - 1)]
    back_send, back_recv = pair_of_sems(returned_view)
    for r in (*rows_out, row):
        for c in other_cols:
            spread(
                [(slabs.at[pl.ds((r * n_col + c) * n_vis, n_vis)], (vis, row, c))],
                across.at[r, col], across_send, return_sems.at[r],
            )
    first_out[...] = dot_tn(packed_out[...], act_out[...])
    for r in (*rows_out, row):
        across[r, col] = slabs[pl.ds((r * n_col + col) * n_vis, n_vis)]
        wait_for(across.at[0, pl.ds(0, n_col - 1)], return_sems.at[r])
        value = across[r, 0].astype(F32)
        for c in range(1, n_col):
            value = value + across[r, c].astype(F32)
        column_sums[r] = value.astype(BF)
        targets = other_vis if r is row else (*other_vis, vis)
        spread([(column_sums.at[r, v], (v, r, col)) for v in targets], returned.at[own], back_send, back_recv)
    o_done()
    block_out[...] = (c_all[pos].astype(F32) + total(o_recv, o_part[pos], group, pos)).astype(BF)
    returned[own] = column_sums[row, vis]
    wait_for(returned_view, back_recv)
    pieces = []
    for i in range(n_vis):
        value = returned[i].astype(F32)
        for r in range(1, n_row):
            value = value + returned[r * n_vis + i].astype(F32)
        pieces.append(value)
    standardized_input = centred * inverse_scale
    slot_out[...] = norm_gradient_pass(
        jnp.concatenate(pieces, axis=1), standardized_input, inverse_scale, gain_row
    )
    for view, sem in sent:
        wait_for(view, sem)


def store_kernel(*refs):
    sources, targets, sems = refs[:4], refs[4:8], refs[8]
    copies = [pltpu.make_async_copy(a, b, sems.at[i]) for i, (a, b) in enumerate(zip(sources, targets))]
    for copy in copies:
        copy.start()
    for copy in copies:
        copy.wait()


def vis_buffers(n_vis, lead, half_rows, width):
    return [
        pltpu.VMEM(lead + (2, half_rows, width), BF),
        pltpu.VMEM(lead + (half_rows, width), BF),
        pltpu.VMEM(lead + (n_vis // 2, half_rows, width), BF),
        pltpu.VMEM(lead + (2, half_rows, width), BF),
    ]


def on_device(
    sizes,
    images,
    counts,
    block_order,
    projector_norm_gain,
    proj_first,
    proj_bias,
    proj_second,
    gate_weight,
    up_weight,
    down_weight,
    cotangent,
):
    n_vis, n_row, n_col = sizes
    group_size = n_row * n_col
    n_dev = n_vis * group_size
    per_device = images.shape[0]
    local_rows = cotangent.shape[0]
    rows = local_rows * group_size
    vf, units = proj_first.shape
    dl, ffl = gate_weight.shape
    hr = rows // 2
    by_group = pltpu.VMEM((group_size, local_rows, dl), BF)
    by_device = pltpu.VMEM((n_dev, per_device, vf), BF)
    n_sends = 3 * (1 + TILES) + 12
    results = pl.pallas_call(
        functools.partial(chain_kernel, sizes),
        out_shape=(
            pltpu.VMEM((local_rows, dl), BF),
            pltpu.VMEM(images.shape, F32),
            pltpu.VMEM((vf, units), F32),
            pltpu.VMEM((units, dl), F32),
        ),
        in_specs=[HBM] * 11,
        out_specs=(VM,) * 4,
        scratch_shapes=[
            pltpu.SMEM(counts.shape, jnp.int32),
            pltpu.SMEM(block_order.shape, jnp.int32),
            pltpu.VMEM(images.shape, BF),
            pltpu.VMEM(projector_norm_gain.shape, F32),
            pltpu.VMEM(cotangent.shape, BF),
            pltpu.VMEM(proj_bias.shape, F32),
            pltpu.VMEM(proj_first.shape, BF),
            pltpu.VMEM(proj_second.shape, BF),
            pltpu.VMEM(gate_weight.shape, BF),
            pltpu.VMEM(up_weight.shape, BF),
            pltpu.VMEM(down_weight.shape, BF),
            pltpu.VMEM((n_vis, per_device, vf), BF),
            by_device,
            by_group,
            pltpu.VMEM((rows, dl), BF),
            by_device,
            pltpu.VMEM((n_row, n_col, n_vis, per_device, vf), BF),
            pltpu.VMEM((n_row, n_vis, per_device, vf), BF),
            pltpu.VMEM((n_row * n_vis, per_device, vf), BF),
            pltpu.VMEM((rows, units), BF),
            pltpu.VMEM((n_vis, rows, units), BF),
            *vis_buffers(n_vis, (), hr, ffl),
            *vis_buffers(n_vis, (TILES,), hr, 2 * ffl // TILES),
            pltpu.VMEM((rows, units), BF),
            pltpu.VMEM((n_vis, rows, units), BF),
            *[by_group] * 8,
            pltpu.VMEM((rows, vf), BF),
            pltpu.VMEM((rows, units), BF),
            pltpu.VMEM((rows, units), BF),
            pltpu.VMEM((rows, dl), BF),
            pltpu.VMEM((rows, units), F32),
            pltpu.VMEM((rows, dl), BF),
            pltpu.VMEM((rows, dl), F32),
            pltpu.VMEM((rows, ffl), BF),
            pltpu.SemaphoreType.DMA((11,)),
            pltpu.SemaphoreType.DMA((n_row,)),
            pltpu.SemaphoreType.DMA((n_row,)),
            pltpu.SemaphoreType.DMA((2 * n_sends,)),
        ],
        compiler_params=pltpu.CompilerParams(
            collective_id=0, has_side_effects=True, vmem_limit_bytes=40 << 20
        ),
    )(
        *[
            pltpu.with_memory_space_constraint(x, pltpu.HBM)
            for x in (
                counts, block_order, images, projector_norm_gain, cotangent,
                proj_bias, proj_first, proj_second, gate_weight, up_weight, down_weight,
            )
        ]
    )
    return pl.pallas_call(
        store_kernel,
        out_shape=tuple(pltpu.HBM(r.shape, r.dtype) for r in results),
        in_specs=[VM] * 4,
        out_specs=(HBM,) * 4,
        scratch_shapes=[pltpu.SemaphoreType.DMA((4,))],
        compiler_params=pltpu.CompilerParams(vmem_limit_bytes=1 << 20),
    )(*[pltpu.with_memory_space_constraint(r, pltpu.VMEM) for r in results])


def solution(mesh):
    in_specs = (
        P(("vis", "row", "col"), None),
        P(),
        P(),
        P(),
        P("vis", ("row", "col")),
        P(("row", "col")),
        P(("row", "col"), "vis"),
        P("vis", ("row", "col")),
        P("vis", ("row", "col")),
        P(("row", "col"), "vis"),
        P(("row", "col"), "vis"),
    )
    out_specs = (
        P(("row", "col"), "vis"),
        P(("vis", "row", "col"), None),
        P("vis", ("row", "col")),
        P(("row", "col"), "vis"),
    )
    sizes = (mesh.shape["vis"], mesh.shape["row"], mesh.shape["col"])
    return jax.shard_map(
        functools.partial(on_device, sizes), mesh=mesh, in_specs=in_specs, out_specs=out_specs, check_vma=False
    )
```

```python
import functools

import jax
import jax.numpy as jnp
from jax import lax
from jax.experimental import pallas as pl
from jax.experimental.pallas import tpu as pltpu
from jax.sharding import PartitionSpec as P


def gelu_parts(pre):
    normal_cdf = 0.5 * (1.0 + jax.scipy.special.erf(pre * 0.7071067811865476))
    density = jnp.exp(-0.5 * pre * pre) * 0.3989422804014327
    return (pre * normal_cdf, normal_cdf + pre * density)


def norm_gradient_pass(gradient_tuple, standardized_input, inverse_scale, projector_norm_gain):
    gain_scaled = gradient_tuple * projector_norm_gain
    return inverse_scale * (
        gain_scaled
        - jnp.mean(gain_scaled, axis=-1, keepdims=True)
        - standardized_input * jnp.mean(gain_scaled * standardized_input, axis=-1, keepdims=True)
    )


def feed_grads(hidden_grad, gate_sum, up_sum, gate_sigmoid):
    gate_grad = (
        hidden_grad * up_sum * gate_sigmoid * (1.0 + gate_sum * (1.0 - gate_sigmoid))
    ).astype(jnp.bfloat16)
    up_grad = (hidden_grad * gate_sum * gate_sigmoid).astype(jnp.bfloat16)
    return (gate_grad, up_grad)


MESH = pl.DeviceIdType.MESH
BF = jnp.bfloat16
F32 = jnp.float32
HBM = pl.BlockSpec(memory_space=pltpu.HBM)
VM = pl.BlockSpec(memory_space=pltpu.VMEM)
HALVES = 2
TILES = 4
LAG = 2
AHEAD = 2


def dot_tn(left, right):
    return lax.dot_general(left, right, (((0,), (0,)), ((), ())), preferred_element_type=F32)


def dot_nt(left, right):
    return lax.dot_general(left, right, (((1,), (1,)), ((), ())), preferred_element_type=F32)


def entry_barrier(devices):
    barrier = pltpu.get_barrier_semaphore()
    for device in devices:
        pl.semaphore_signal(barrier, inc=1, device_id=device, device_id_type=MESH)
    return barrier


def far_first(me, n):
    upper = 2 * me // n
    order = []
    for j in range(n - 1):
        down = n - 1 - j
        down = down - (me - down + n) // n
        up = j + (j - me + n) // n
        order.append(upper * up + (1 - upper) * down)
    return order


def spread(targets, dst, send_sem, recv_sem):
    for src, device in targets:
        pltpu.make_async_remote_copy(
            src_ref=src,
            dst_ref=dst,
            send_sem=send_sem,
            recv_sem=recv_sem,
            device_id=device,
            device_id_type=MESH,
        ).start()


def wait_for(view, sem):
    pltpu.make_async_copy(view, view, sem).wait()


def my_place(sizes):
    n_vis, _, n_col = sizes
    vis, row, col = lax.axis_index("vis"), lax.axis_index("row"), lax.axis_index("col")
    return vis, row, col, (row * n_col + col) * n_vis + vis


def row_places(counts, order, n_vis, per, group, rows, shape, axis):
    slots = lax.broadcasted_iota(jnp.int32, shape, axis)
    owner = slots // per % n_vis
    offset = slots // (n_vis * per) * per + slots % per
    start_of = jnp.zeros(shape, jnp.int32)
    count_of = jnp.zeros(shape, jnp.int32)
    begin = jnp.int32(0)
    for b in range(n_vis):
        device = order[b]
        live_rows = counts[device]
        start_of = jnp.where(owner == device, begin, start_of)
        count_of = jnp.where(owner == device, live_rows, count_of)
        begin = begin + live_rows
    language = start_of + offset
    owned = rows // group
    gr = owned // HALVES
    working = language % owned // gr * (rows // HALVES) + language // owned * gr + language % gr
    return jnp.where(offset < count_of, working, -1)


def chain_kernel(
    sizes, counts_hbm, order_hbm, images_hbm, gain_hbm, cot_hbm, bias_hbm,
    wf_hbm, ws_hbm, wg_hbm, wu_hbm, wd_hbm,
    block_out, slot_out, first_out, second_out,
    counts, order, images, gain, cot, bias, wf, ws, wg, wu, wd,
    blocks, rows_all, cot_mine, cot_all, upstream, slabs, across, column_sums, returned, direct,
    b_part, b_recv, h_part, h_pair, h_ring, h_all,
    d_part, d_pair, d_ring, d_all, f_part, f_recv,
    c_part, c_recv, c_all, e_part, e_recv, e_all, o_part, o_recv,
    packed_out, act_out, hid_out, ig_out, slope, inputs, acc, hidden, wsem, gather_sems, return_sems, sems,
):
    n_vis, n_row, n_col = sizes
    group = n_row * n_col
    n_dev = n_vis * group
    vis, row, col, me = my_place(sizes)
    pos = row * n_col + col
    core, ring_at, n_ring = lax.rem(vis, 2), vis // 2, n_vis // 2
    per, vf = blocks.shape[1:]
    rows, dl = upstream.shape
    hr = rows // HALVES
    gr = hr // group
    halves = [slice(h * hr, (h + 1) * hr) for h in range(HALVES)]
    ffl = wg.shape[1]
    tw = ffl // TILES

    def in_ring(p):
        return (2 * p + core, row, col)

    rows_out = far_first(row, n_row)
    other_cols = [lax.rem(col + j, n_col) for j in range(1, n_col)]
    other_vis = [
        (2 * lax.rem(ring_at + k, n_ring) + side) for k in range(1, n_ring) for side in (1 - core, core)
    ] + [2 * ring_at + 1 - core]
    group_order = [(r, c) for r in rows_out for c in (*other_cols, col)] + [(row, c) for c in other_cols]
    all_vis = (*other_vis, vis)
    row_mates = [(v, row, c) for c in other_cols for v in all_vis]
    mates = [(v, row, col) for v in other_vis] + [(v, r, col) for r in rows_out for v in (*other_vis, vis)]

    loads = {}
    for i, (name, src, dst) in enumerate(
        (
            ("images", images_hbm, images), ("gain", gain_hbm, gain), ("cot", cot_hbm, cot),
            ("bias", bias_hbm, bias), ("counts", counts_hbm, counts), ("order", order_hbm, order),
            ("wd", wd_hbm, wd), ("wf", wf_hbm, wf), ("ws", ws_hbm, ws), ("wg", wg_hbm, wg), ("wu", wu_hbm, wu),
        )
    ):
        loads[name] = pltpu.make_async_copy(src, dst, wsem.at[i])
        loads[name].start()
    neighbours = mates + [(vis, r, c) for r in rows_out for c in other_cols] + row_mates
    barrier = entry_barrier(neighbours)

    sent = []

    def pair_of_sems(view):
        idx = 2 * len(sent)
        sent.append((view, sems.at[idx]))
        return sems.at[idx], sems.at[idx + 1]

    def start(targets, dst, n, at):
        view = dst.at[pl.ds(0, n - 1)]
        send_sem, recv_sem = pair_of_sems(view)
        spread(targets, dst.at[at], send_sem, recv_sem)
        return lambda: wait_for(view, recv_sem)

    def scatter(part, recv):
        return start([(part.at[r * n_col + c], (vis, r, c)) for r, c in group_order], recv, group, pos)

    def gather(mine, everything):
        return start([(mine, (vis, r, c)) for r, c in group_order], everything, group, pos)

    def share(part, recv):
        return start([(part, (v, row, col)) for v in other_vis], recv, n_vis, vis)

    def to_partner(src, dst):
        send_sem, recv_sem = pair_of_sems(dst)
        pltpu.make_async_remote_copy(
            src_ref=src, dst_ref=dst, send_sem=send_sem, recv_sem=recv_sem,
            device_id=(2 * ring_at + 1 - core, row, col), device_id_type=MESH,
        ).start()
        return lambda: wait_for(dst, recv_sem)

    def vis_begin(part, pair):
        return to_partner(part.at[1 - core], pair)

    def vis_middle(arrived, part, pair, ring):
        arrived()
        ring[ring_at] = (part[core].astype(F32) + pair[...].astype(F32)).astype(BF)
        others = [in_ring(lax.rem(ring_at + k, n_ring)) for k in range(1, n_ring)]
        return start([(ring.at[ring_at], device) for device in others], ring, n_ring, ring_at)

    def vis_finish(arrived, ring, result):
        arrived()
        value = ring[0].astype(F32)
        for i in range(1, n_ring):
            value = value + ring[i].astype(F32)
        result[core] = value.astype(BF)
        return to_partner(result.at[core], result.at[core])

    def by_owner(value):
        return value.astype(BF).reshape(group, gr, value.shape[1])

    def total(recv, own, n, at):
        recv[at] = own
        result = recv[0].astype(F32)
        for i in range(1, n):
            result = result + recv[i].astype(F32)
        return result

    def whole(buf, n):
        return jnp.concatenate([buf[i].astype(F32) for i in range(n)], axis=0)

    loads["images"].wait()
    loads["gain"].wait()
    gain_row = gain[...].reshape(1, gain.shape[0])
    values = images[...].astype(F32)
    centred = values - jnp.mean(values, axis=-1, keepdims=True)
    inverse_scale = lax.rsqrt(jnp.mean(centred * centred, axis=-1, keepdims=True) + 1e-05)
    normed = centred * inverse_scale * gain_row
    for i in range(n_vis):
        blocks[i] = normed[:, i * vf:(i + 1) * vf].astype(BF)
    for name in ("cot", "bias", "counts", "order"):
        loads[name].wait()
    pl.semaphore_wait(barrier, len(neighbours))
    own = row * n_vis + vis
    mates_view = rows_all.at[pl.ds(0, len(mates))]
    send_sem, _ = pair_of_sems(mates_view)
    spread([(blocks.at[d[0]], d) for d in mates], rows_all.at[me], send_sem, gather_sems.at[row])
    forward_view = rows_all.at[pl.ds(0, n_row * n_vis * (n_col - 1))]
    forward_send, forward_recv = pair_of_sems(forward_view)
    spread([(blocks.at[v], (v, row, c)) for c in other_cols for v in all_vis], rows_all.at[me], forward_send, forward_recv)
    rows_all[me] = blocks[vis]
    for r in rows_out[::-1]:
        wait_for(rows_all.at[pl.ds(0, n_vis)], gather_sems.at[r])
        chunk = rows_all.at[pl.ds((r * n_col + col) * n_vis, n_vis)]
        spread([(chunk, (vis, row, c)) for c in other_cols], chunk, forward_send, forward_recv)
    n_slots = n_dev * per
    place = row_places(counts, order, n_vis, per, group, rows, (rows, n_slots), 1)
    pick = jnp.where(place == lax.broadcasted_iota(jnp.int32, (rows, n_slots), 0), 1.0, 0.0).astype(BF)

    loads["wf"].wait()
    wait_for(rows_all.at[pl.ds(0, n_vis - 1)], gather_sems.at[row])
    wait_for(forward_view, forward_recv)
    packed_out[...] = jnp.dot(
        pick, rows_all[...].reshape(n_slots, vf), preferred_element_type=F32
    ).astype(BF)
    b_done = []
    for h, half in enumerate(halves):
        b_part[h] = jnp.dot(packed_out[half], wf[...], preferred_element_type=F32).astype(BF)
        b_done.append(share(b_part.at[h], b_recv.at[h]))
    cot_mine[...] = cot[...].reshape(HALVES, gr, dl)
    cot_done = gather(cot_mine, cot_all)
    cot_all[pos] = cot_mine[...]
    loads["ws"].wait()
    c_done = []
    for h, half in enumerate(halves):
        b_done[h]()
        pre = total(b_recv.at[h], b_part[h], n_vis, vis) + bias[...].reshape(1, bias.shape[0])
        activated, slope_value = gelu_parts(pre)
        slope[half] = slope_value
        hid_out[half] = activated.astype(BF)
        c_part[h] = by_owner(jnp.dot(hid_out[half], ws[...], preferred_element_type=F32))
        c_done.append(scatter(c_part.at[h], c_recv.at[h]))

    cot_done()
    for h, half in enumerate(halves):
        upstream[half] = cot_all[:, h].reshape(hr, dl)
    loads["wd"].wait()
    mid = rows // 2
    hw = ffl // 8
    for t in range(8):
        cols = slice(t * hw, (t + 1) * hw)
        value = dot_nt(upstream[...], wd[cols, :])
        for i in range(2):
            h_part[i, :, cols] = value[i * mid:(i + 1) * mid].astype(BF)
    h_done = vis_begin(h_part, h_pair)
    h_done = vis_middle(h_done, h_part, h_pair, h_ring)
    for h in range(HALVES):
        c_done[h]()
        c_all[h, pos] = total(c_recv.at[h], c_part[h, pos], group, pos).astype(BF)
        c_done[h] = gather(c_all.at[h, pos], c_all.at[h])
    loads["wg"].wait()
    loads["wu"].wait()
    h_done = vis_finish(h_done, h_ring, h_all)

    steps = [(h, t) for h in range(HALVES) for t in range(TILES)]
    d_done = {}
    hc = hr // 2

    def d_middle(k):
        d_done[k] = vis_middle(d_done[k], d_part.at[k], d_pair.at[k], d_ring.at[k])

    def d_finish(k):
        d_done[k] = vis_finish(d_done[k], d_ring.at[k], d_all.at[k])

    for i, (h, t) in enumerate(steps):
        if t == 0:
            c_done[h]()
            inputs[halves[h]] = c_all[h].reshape(hr, dl)
        cols = slice(t * tw, (t + 1) * tw)
        for part, weight in enumerate((wg, wu)):
            value = jnp.dot(inputs[halves[h]], weight[:, cols], preferred_element_type=F32)
            for k in range(2):
                d_part[h, t, k, :, part * tw:(part + 1) * tw] = value[k * hc:(k + 1) * hc].astype(BF)
        d_done[h, t] = vis_begin(d_part.at[h, t], d_pair.at[h, t])
        if i >= LAG:
            d_middle(steps[i - LAG])
    for k in steps[-LAG:]:
        d_middle(k)
    for k in steps[:AHEAD]:
        d_finish(k)
    h_done()
    e_done = []
    for i, (h, t) in enumerate(steps):
        if i + AHEAD < len(steps):
            d_finish(steps[i + AHEAD])
        d_done[h, t]()
        cols = slice(t * tw, (t + 1) * tw)
        both = whole(d_all.at[h, t], 2)
        gate_sum, up_sum = both[:, :tw], both[:, tw:]
        hidden_grad = whole(h_all.at[:, :, cols], 2) if HALVES == 1 else h_all[h, :, cols].astype(F32)
        gate_sigmoid = jax.nn.sigmoid(gate_sum)
        hidden[halves[h], cols] = (gate_sum * gate_sigmoid * up_sum).astype(BF)
        gate_grad, up_grad = feed_grads(hidden_grad, gate_sum, up_sum, gate_sigmoid)
        value = dot_nt(gate_grad, wg[:, cols]) + dot_nt(up_grad, wu[:, cols])
        if t == 0:
            acc[...] = value
        elif t < TILES - 1:
            acc[...] += value
        else:
            e_part[h] = by_owner(acc[...] + value)
            e_done.append(scatter(e_part.at[h], e_recv.at[h]))
    value = jnp.dot(hidden[...], wd[...], preferred_element_type=F32)
    for h, half in enumerate(halves):
        o_part[:, h] = by_owner(value[half])
    place = row_places(counts, order, n_vis, per, group, rows, (n_slots, rows), 0)
    put = jnp.where(place == lax.broadcasted_iota(jnp.int32, (n_slots, rows), 1), 1.0, 0.0).astype(BF)
    for h in range(HALVES):
        e_done[h]()
        e_all[h, pos] = (total(e_recv.at[h], e_part[h, pos], group, pos) + cot_mine[h].astype(F32)).astype(BF)
        e_done[h] = gather(e_all.at[h, pos], e_all.at[h])
    f_done = []
    for h, half in enumerate(halves):
        e_done[h]()
        ig_out[half] = e_all[h].reshape(hr, dl)
        f_part[h] = dot_nt(ig_out[half], ws[...]).astype(BF)
        f_done.append(share(f_part.at[h], f_recv.at[h]))
    o_done = scatter(o_part, o_recv)
    second_out[...] = dot_tn(hid_out[...], ig_out[...])
    for h, half in enumerate(halves):
        f_done[h]()
        act_out[half] = (total(f_recv.at[h], f_part[h], n_vis, vis) * slope[half]).astype(BF)

    slot_act = jnp.dot(put, act_out[...], preferred_element_type=F32).astype(BF)
    slabs[...] = dot_nt(slot_act, wf[...]).astype(BF).reshape(n_dev, per, vf)
    across_send, _ = pair_of_sems(slabs.at[pl.ds(0, (n_row - 1) * n_vis * (n_col - 1))])
    direct_view = direct.at[pl.ds(0, n_vis * n_col - 1)]
    direct_send, direct_recv = pair_of_sems(direct_view)
    returned_view = returned.at[pl.ds(0, (n_row - 1) * n_vis)]
    back_send, back_recv = pair_of_sems(returned_view)
    for r in rows_out:
        for c in other_cols:
            spread(
                [(slabs.at[pl.ds((r * n_col + c) * n_vis, n_vis)], (vis, row, c))],
                across.at[r, col], across_send, return_sems.at[r],
            )
    spread(
        [(slabs.at[(row * n_col + c) * n_vis + v], (v, row, c)) for v, _, c in row_mates + mates[:n_vis - 1]],
        direct.at[col * n_vis + vis], direct_send, direct_recv,
    )
    first_out[...] = dot_tn(packed_out[...], act_out[...])
    for r in rows_out:
        across[r, col] = slabs[pl.ds((r * n_col + col) * n_vis, n_vis)]
        wait_for(across.at[0, pl.ds(0, n_col - 1)], return_sems.at[r])
        value = across[r, 0].astype(F32)
        for c in range(1, n_col):
            value = value + across[r, c].astype(F32)
        column_sums[r] = value.astype(BF)
        spread([(column_sums.at[r, v], (v, r, col)) for v in all_vis], returned.at[own], back_send, back_recv)
    o_done()
    o_sum = total(o_recv, o_part[pos], group, pos)
    block_out[...] = jnp.concatenate([o_sum[h] + c_all[h, pos].astype(F32) for h in range(HALVES)], axis=0).astype(BF)
    direct[col * n_vis + vis] = slabs[me]
    wait_for(direct_view, direct_recv)
    for i in range(n_vis):
        value = direct[i].astype(F32)
        for c in range(1, n_col):
            value = value + direct[c * n_vis + i].astype(F32)
        returned[row * n_vis + i] = value.astype(BF)
    wait_for(returned_view, back_recv)
    pieces = []
    for i in range(n_vis):
        value = returned[i].astype(F32)
        for r in range(1, n_row):
            value = value + returned[r * n_vis + i].astype(F32)
        pieces.append(value)
    standardized_input = centred * inverse_scale
    slot_out[...] = norm_gradient_pass(
        jnp.concatenate(pieces, axis=1), standardized_input, inverse_scale, gain_row
    )
    for view, sem in sent:
        wait_for(view, sem)


def store_kernel(*refs):
    sources, targets, sems = refs[:4], refs[4:8], refs[8]
    copies = [pltpu.make_async_copy(a, b, sems.at[i]) for i, (a, b) in enumerate(zip(sources, targets))]
    for copy in copies:
        copy.start()
    for copy in copies:
        copy.wait()


def vis_buffers(n_vis, lead, half_rows, width):
    return [
        pltpu.VMEM(lead + (2, half_rows, width), BF),
        pltpu.VMEM(lead + (half_rows, width), BF),
        pltpu.VMEM(lead + (n_vis // 2, half_rows, width), BF),
        pltpu.VMEM(lead + (2, half_rows, width), BF),
    ]


def on_device(
    sizes,
    images,
    counts,
    block_order,
    projector_norm_gain,
    proj_first,
    proj_bias,
    proj_second,
    gate_weight,
    up_weight,
    down_weight,
    cotangent,
):
    n_vis, n_row, n_col = sizes
    group_size = n_row * n_col
    n_dev = n_vis * group_size
    per_device = images.shape[0]
    local_rows = cotangent.shape[0]
    rows = local_rows * group_size
    vf, units = proj_first.shape
    dl, ffl = gate_weight.shape
    hr = rows // HALVES
    gr = local_rows // HALVES
    by_group = pltpu.VMEM((HALVES, group_size, gr, dl), BF)
    owned_halves = pltpu.VMEM((group_size, HALVES, gr, dl), BF)
    by_device = pltpu.VMEM((n_dev, per_device, vf), BF)
    n_sends = 3 * (1 + HALVES * TILES) + 6 * HALVES + 7
    results = pl.pallas_call(
        functools.partial(chain_kernel, sizes),
        out_shape=(
            pltpu.VMEM((local_rows, dl), BF),
            pltpu.VMEM(images.shape, F32),
            pltpu.VMEM((vf, units), F32),
            pltpu.VMEM((units, dl), F32),
        ),
        in_specs=[HBM] * 11,
        out_specs=(VM,) * 4,
        scratch_shapes=[
            pltpu.SMEM(counts.shape, jnp.int32),
            pltpu.SMEM(block_order.shape, jnp.int32),
            pltpu.VMEM(images.shape, BF),
            pltpu.VMEM(projector_norm_gain.shape, F32),
            pltpu.VMEM(cotangent.shape, BF),
            pltpu.VMEM(proj_bias.shape, F32),
            pltpu.VMEM(proj_first.shape, BF),
            pltpu.VMEM(proj_second.shape, BF),
            pltpu.VMEM(gate_weight.shape, BF),
            pltpu.VMEM(up_weight.shape, BF),
            pltpu.VMEM(down_weight.shape, BF),
            pltpu.VMEM((n_vis, per_device, vf), BF),
            by_device,
            pltpu.VMEM((HALVES, gr, dl), BF),
            owned_halves,
            pltpu.VMEM((rows, dl), BF),
            by_device,
            pltpu.VMEM((n_row, n_col, n_vis, per_device, vf), BF),
            pltpu.VMEM((n_row, n_vis, per_device, vf), BF),
            pltpu.VMEM((n_row * n_vis, per_device, vf), BF),
            pltpu.VMEM((n_col * n_vis, per_device, vf), BF),
            pltpu.VMEM((HALVES, hr, units), BF),
            pltpu.VMEM((HALVES, n_vis, hr, units), BF),
            *vis_buffers(n_vis, (), rows // 2, ffl),
            *vis_buffers(n_vis, (HALVES, TILES), hr // 2, 2 * ffl // TILES),
            pltpu.VMEM((HALVES, hr, units), BF),
            pltpu.VMEM((HALVES, n_vis, hr, units), BF),
            *[by_group] * 6,
            owned_halves,
            owned_halves,
            pltpu.VMEM((rows, vf), BF),
            pltpu.VMEM((rows, units), BF),
            pltpu.VMEM((rows, units), BF),
            pltpu.VMEM((rows, dl), BF),
            pltpu.VMEM((rows, units), F32),
            pltpu.VMEM((rows, dl), BF),
            pltpu.VMEM((hr, dl), F32),
            pltpu.VMEM((rows, ffl), BF),
            pltpu.SemaphoreType.DMA((11,)),
            pltpu.SemaphoreType.DMA((n_row,)),
            pltpu.SemaphoreType.DMA((n_row,)),
            pltpu.SemaphoreType.DMA((2 * n_sends,)),
        ],
        compiler_params=pltpu.CompilerParams(
            collective_id=0, has_side_effects=True, vmem_limit_bytes=40 << 20
        ),
    )(
        *[
            pltpu.with_memory_space_constraint(x, pltpu.HBM)
            for x in (
                counts, block_order, images, projector_norm_gain, cotangent,
                proj_bias, proj_first, proj_second, gate_weight, up_weight, down_weight,
            )
        ]
    )
    return pl.pallas_call(
        store_kernel,
        out_shape=tuple(pltpu.HBM(r.shape, r.dtype) for r in results),
        in_specs=[VM] * 4,
        out_specs=(HBM,) * 4,
        scratch_shapes=[pltpu.SemaphoreType.DMA((4,))],
        compiler_params=pltpu.CompilerParams(vmem_limit_bytes=1 << 20),
    )(*[pltpu.with_memory_space_constraint(r, pltpu.VMEM) for r in results])


def solution(mesh):
    in_specs = (
        P(("vis", "row", "col"), None),
        P(),
        P(),
        P(),
        P("vis", ("row", "col")),
        P(("row", "col")),
        P(("row", "col"), "vis"),
        P("vis", ("row", "col")),
        P("vis", ("row", "col")),
        P(("row", "col"), "vis"),
        P(("row", "col"), "vis"),
    )
    out_specs = (
        P(("row", "col"), "vis"),
        P(("vis", "row", "col"), None),
        P("vis", ("row", "col")),
        P(("row", "col"), "vis"),
    )
    sizes = (mesh.shape["vis"], mesh.shape["row"], mesh.shape["col"])
    return jax.shard_map(
        functools.partial(on_device, sizes), mesh=mesh, in_specs=in_specs, out_specs=out_specs, check_vma=False
    )
```

```python
import functools

import jax
import jax.numpy as jnp
from jax import lax
from jax.experimental import pallas as pl
from jax.experimental.pallas import tpu as pltpu
from jax.sharding import PartitionSpec as P


def gelu_parts(pre):
    normal_cdf = 0.5 * (1.0 + jax.scipy.special.erf(pre * 0.7071067811865476))
    density = jnp.exp(-0.5 * pre * pre) * 0.3989422804014327
    return (pre * normal_cdf, normal_cdf + pre * density)


def norm_gradient_pass(gradient_tuple, standardized_input, inverse_scale, projector_norm_gain):
    gain_scaled = gradient_tuple * projector_norm_gain
    return inverse_scale * (
        gain_scaled
        - jnp.mean(gain_scaled, axis=-1, keepdims=True)
        - standardized_input * jnp.mean(gain_scaled * standardized_input, axis=-1, keepdims=True)
    )


def feed_grads(hidden_grad, gate_sum, up_sum, gate_sigmoid):
    gate_grad = (
        hidden_grad * up_sum * gate_sigmoid * (1.0 + gate_sum * (1.0 - gate_sigmoid))
    ).astype(jnp.bfloat16)
    up_grad = (hidden_grad * gate_sum * gate_sigmoid).astype(jnp.bfloat16)
    return (gate_grad, up_grad)


MESH = pl.DeviceIdType.MESH
BF = jnp.bfloat16
F32 = jnp.float32
HBM = pl.BlockSpec(memory_space=pltpu.HBM)
VM = pl.BlockSpec(memory_space=pltpu.VMEM)
HALVES = 2
TILES = 4
LAG = 2
AHEAD = 2
FLIPS = 8


def product(left, right):
    return jnp.dot(left, right, preferred_element_type=F32)


def dot_tn(left, right):
    return lax.dot_general(left, right, (((0,), (0,)), ((), ())), preferred_element_type=F32)


def dot_nt(left, right):
    return lax.dot_general(left, right, (((1,), (1,)), ((), ())), preferred_element_type=F32)


def entry_barrier(devices):
    barrier = pltpu.get_barrier_semaphore()
    for device in devices:
        pl.semaphore_signal(barrier, inc=1, device_id=device, device_id_type=MESH)
    return barrier


def far_first(me, n):
    upper = 2 * me // n
    order = []
    for j in range(n - 1):
        down = n - 1 - j
        down = down - (me - down + n) // n
        up = j + (j - me + n) // n
        order.append(upper * up + (1 - upper) * down)
    return order


def spread(targets, dst, send_sem, recv_sem):
    for src, device in targets:
        pltpu.make_async_remote_copy(
            src_ref=src,
            dst_ref=dst,
            send_sem=send_sem,
            recv_sem=recv_sem,
            device_id=device,
            device_id_type=MESH,
        ).start()


def wait_for(view, sem):
    pltpu.make_async_copy(view, view, sem).wait()


def my_place(sizes):
    n_vis, _, n_col = sizes
    vis, row, col = lax.axis_index("vis"), lax.axis_index("row"), lax.axis_index("col")
    return vis, row, col, (row * n_col + col) * n_vis + vis


def row_places(counts, order, n_vis, per, group, rows, shape, axis):
    slots = lax.broadcasted_iota(jnp.int32, shape, axis)
    owner = slots // per % n_vis
    offset = slots // (n_vis * per) * per + slots % per
    start_of = jnp.zeros(shape, jnp.int32)
    count_of = jnp.zeros(shape, jnp.int32)
    begin = jnp.int32(0)
    for b in range(n_vis):
        device = order[b]
        live_rows = counts[device]
        start_of = jnp.where(owner == device, begin, start_of)
        count_of = jnp.where(owner == device, live_rows, count_of)
        begin = begin + live_rows
    language = start_of + offset
    owned = rows // group
    gr = owned // HALVES
    working = language % owned // gr * (rows // HALVES) + language // owned * gr + language % gr
    return jnp.where(offset < count_of, working, -1)


def chain_kernel(
    sizes, counts_hbm, order_hbm, images_hbm, gain_hbm, cot_hbm, bias_hbm,
    wf_hbm, ws_hbm, wg_hbm, wu_hbm, wd_hbm,
    block_out, slot_out, first_out, second_out,
    counts, order, images, gain, cot, bias, wf, ws, wg, wu, wd, wgt, wut, wst, wft,
    blocks, rows_all, cot_mine, cot_all, upstream, slabs, across, column_sums, returned, direct,
    b_part, b_recv, h_part, h_pair, h_ring, h_all,
    d_part, d_pair, d_ring, d_all, f_part, f_recv,
    c_part, c_recv, c_all, e_part, e_recv, e_all, o_part, o_recv,
    packed_out, act_out, hid_out, ig_out, slope, inputs, acc, hidden, wsem, gather_sems, return_sems, sems,
):
    n_vis, n_row, n_col = sizes
    group = n_row * n_col
    n_dev = n_vis * group
    vis, row, col, me = my_place(sizes)
    pos = row * n_col + col
    core, ring_at, n_ring = lax.rem(vis, 2), vis // 2, n_vis // 2
    per, vf = blocks.shape[1:]
    rows, dl = upstream.shape
    hr = rows // HALVES
    gr = hr // group
    halves = [slice(h * hr, (h + 1) * hr) for h in range(HALVES)]
    ffl = wg.shape[1]
    tw = ffl // TILES

    def in_ring(p):
        return (2 * p + core, row, col)

    rows_out = far_first(row, n_row)
    other_cols = [lax.rem(col + j, n_col) for j in range(1, n_col)]
    other_vis = [
        (2 * lax.rem(ring_at + k, n_ring) + side) for k in range(1, n_ring) for side in (1 - core, core)
    ] + [2 * ring_at + 1 - core]
    group_order = [(r, c) for r in rows_out for c in (*other_cols, col)] + [(row, c) for c in other_cols]
    all_vis = (*other_vis, vis)
    row_mates = [(v, row, c) for c in other_cols for v in all_vis]
    mates = [(v, row, col) for v in other_vis] + [(v, r, col) for r in rows_out[::-1] for v in (*other_vis, vis)]

    loads = {}
    for i, (name, src, dst) in enumerate(
        (
            ("images", images_hbm, images), ("gain", gain_hbm, gain), ("cot", cot_hbm, cot),
            ("bias", bias_hbm, bias), ("counts", counts_hbm, counts), ("order", order_hbm, order),
            ("wd", wd_hbm, wd), ("wf", wf_hbm, wf), ("ws", ws_hbm, ws), ("wg", wg_hbm, wg), ("wu", wu_hbm, wu),
        )
    ):
        loads[name] = pltpu.make_async_copy(src, dst, wsem.at[i])
        loads[name].start()
    neighbours = mates + [(vis, r, c) for r in rows_out for c in other_cols] + row_mates
    barrier = entry_barrier(neighbours)

    sent = []

    def pair_of_sems(view):
        idx = 2 * len(sent)
        sent.append((view, sems.at[idx]))
        return sems.at[idx], sems.at[idx + 1]

    def start(targets, dst, n, at):
        view = dst.at[pl.ds(0, n - 1)]
        send_sem, recv_sem = pair_of_sems(view)
        spread(targets, dst.at[at], send_sem, recv_sem)
        return lambda: wait_for(view, recv_sem)

    def scatter(part, recv):
        return start([(part.at[r * n_col + c], (vis, r, c)) for r, c in group_order], recv, group, pos)

    def gather(mine, everything):
        return start([(mine, (vis, r, c)) for r, c in group_order], everything, group, pos)

    def share(part, recv):
        return start([(part, (v, row, col)) for v in other_vis], recv, n_vis, vis)

    def to_partner(src, dst):
        send_sem, recv_sem = pair_of_sems(dst)
        pltpu.make_async_remote_copy(
            src_ref=src, dst_ref=dst, send_sem=send_sem, recv_sem=recv_sem,
            device_id=(2 * ring_at + 1 - core, row, col), device_id_type=MESH,
        ).start()
        return lambda: wait_for(dst, recv_sem)

    def vis_begin(part, pair):
        return to_partner(part.at[1 - core], pair)

    def vis_middle(arrived, part, pair, ring):
        arrived()
        ring[ring_at] = (part[core].astype(F32) + pair[...].astype(F32)).astype(BF)
        others = [in_ring(lax.rem(ring_at + k, n_ring)) for k in range(1, n_ring)]
        return start([(ring.at[ring_at], device) for device in others], ring, n_ring, ring_at)

    def vis_finish(arrived, ring, result):
        arrived()
        value = ring[0].astype(F32)
        for i in range(1, n_ring):
            value = value + ring[i].astype(F32)
        result[core] = value.astype(BF)
        return to_partner(result.at[core], result.at[core])

    def by_owner(value):
        return value.astype(BF).reshape(group, gr, value.shape[1])

    def total(recv, own, n, at):
        recv[at] = own
        result = recv[0].astype(F32)
        for i in range(1, n):
            result = result + recv[i].astype(F32)
        return result

    def whole(buf, n):
        return jnp.concatenate([buf[i].astype(F32) for i in range(n)], axis=0)

    loads["images"].wait()
    loads["gain"].wait()
    gain_row = gain[...].reshape(1, gain.shape[0])
    values = images[...].astype(F32)
    centred = values - jnp.mean(values, axis=-1, keepdims=True)
    inverse_scale = lax.rsqrt(jnp.mean(centred * centred, axis=-1, keepdims=True) + 1e-05)
    normed = centred * inverse_scale * gain_row
    for i in range(n_vis):
        blocks[i] = normed[:, i * vf:(i + 1) * vf].astype(BF)
    for name in ("cot", "bias", "counts", "order"):
        loads[name].wait()
    pl.semaphore_wait(barrier, len(neighbours))
    own = row * n_vis + vis
    mates_view = rows_all.at[pl.ds(0, len(mates))]
    send_sem, _ = pair_of_sems(mates_view)
    spread([(blocks.at[d[0]], d) for d in mates], rows_all.at[me], send_sem, gather_sems.at[row])
    forward_view = rows_all.at[pl.ds(0, n_row * n_vis * (n_col - 1))]
    forward_send, forward_recv = pair_of_sems(forward_view)
    spread([(blocks.at[v], (v, row, c)) for c in other_cols for v in all_vis], rows_all.at[me], forward_send, forward_recv)
    rows_all[me] = blocks[vis]
    flips = [(a, b, slice(t * ffl // FLIPS, (t + 1) * ffl // FLIPS)) for t in range(FLIPS) for a, b in ((wg, wgt), (wu, wut))]
    flips_each = len(flips) // n_row
    for i, r in enumerate(rows_out[::-1]):
        wait_for(rows_all.at[pl.ds(0, n_vis)], gather_sems.at[r])
        chunk = rows_all.at[pl.ds((r * n_col + col) * n_vis, n_vis)]
        spread([(chunk, (vis, row, c)) for c in other_cols], chunk, forward_send, forward_recv)
        if i == 0:
            loads["wg"].wait()
            loads["wu"].wait()
        for source, target, band in flips[i * flips_each:(i + 1) * flips_each]:
            target[band, :] = source[:, band].T
    for source, target, band in flips[(n_row - 1) * flips_each:]:
        target[band, :] = source[:, band].T
    n_slots = n_dev * per
    place = row_places(counts, order, n_vis, per, group, rows, (rows, n_slots), 1)
    pick = jnp.where(place == lax.broadcasted_iota(jnp.int32, (rows, n_slots), 0), 1.0, 0.0).astype(BF)

    loads["wf"].wait()
    wait_for(rows_all.at[pl.ds(0, n_vis - 1)], gather_sems.at[row])
    wait_for(forward_view, forward_recv)
    packed_out[...] = jnp.dot(
        pick, rows_all[...].reshape(n_slots, vf), preferred_element_type=F32
    ).astype(BF)
    b_done = []
    for h, half in enumerate(halves):
        b_part[h] = jnp.dot(packed_out[half], wf[...], preferred_element_type=F32).astype(BF)
        b_done.append(share(b_part.at[h], b_recv.at[h]))
    cot_mine[...] = cot[...].reshape(HALVES, gr, dl)
    cot_done = gather(cot_mine, cot_all)
    cot_all[pos] = cot_mine[...]
    loads["ws"].wait()
    c_done = []
    for h, half in enumerate(halves):
        b_done[h]()
        pre = total(b_recv.at[h], b_part[h], n_vis, vis) + bias[...].reshape(1, bias.shape[0])
        activated, slope_value = gelu_parts(pre)
        slope[half] = slope_value
        hid_out[half] = activated.astype(BF)
        c_part[h] = by_owner(jnp.dot(hid_out[half], ws[...], preferred_element_type=F32))
        c_done.append(scatter(c_part.at[h], c_recv.at[h]))

    cot_done()
    for h, half in enumerate(halves):
        upstream[half] = cot_all[:, h].reshape(hr, dl)
    loads["wd"].wait()
    mid = rows // 2
    hw = ffl // 8
    for t in range(8):
        cols = slice(t * hw, (t + 1) * hw)
        value = dot_nt(upstream[...], wd[cols, :])
        for i in range(2):
            h_part[i, :, cols] = value[i * mid:(i + 1) * mid].astype(BF)
    h_done = vis_begin(h_part, h_pair)
    h_done = vis_middle(h_done, h_part, h_pair, h_ring)
    for h in range(HALVES):
        c_done[h]()
        c_all[h, pos] = total(c_recv.at[h], c_part[h, pos], group, pos).astype(BF)
        c_done[h] = gather(c_all.at[h, pos], c_all.at[h])
    wst[...] = ws[...].T
    wft[...] = wf[...].T
    h_done = vis_finish(h_done, h_ring, h_all)

    steps = [(h, t) for h in range(HALVES) for t in range(TILES)]
    d_done = {}
    hc = hr // 2

    def d_middle(k):
        d_done[k] = vis_middle(d_done[k], d_part.at[k], d_pair.at[k], d_ring.at[k])

    def d_finish(k):
        d_done[k] = vis_finish(d_done[k], d_ring.at[k], d_all.at[k])

    for i, (h, t) in enumerate(steps):
        if t == 0:
            c_done[h]()
            inputs[halves[h]] = c_all[h].reshape(hr, dl)
        cols = slice(t * tw, (t + 1) * tw)
        for part, weight in enumerate((wg, wu)):
            value = jnp.dot(inputs[halves[h]], weight[:, cols], preferred_element_type=F32)
            for k in range(2):
                d_part[h, t, k, :, part * tw:(part + 1) * tw] = value[k * hc:(k + 1) * hc].astype(BF)
        d_done[h, t] = vis_begin(d_part.at[h, t], d_pair.at[h, t])
        if i >= LAG:
            d_middle(steps[i - LAG])
    for k in steps[-LAG:]:
        d_middle(k)
    for k in steps[:AHEAD]:
        d_finish(k)
    h_done()
    e_done = []
    for i, (h, t) in enumerate(steps):
        if i + AHEAD < len(steps):
            d_finish(steps[i + AHEAD])
        d_done[h, t]()
        cols = slice(t * tw, (t + 1) * tw)
        both = whole(d_all.at[h, t], 2)
        gate_sum, up_sum = both[:, :tw], both[:, tw:]
        hidden_grad = whole(h_all.at[:, :, cols], 2) if HALVES == 1 else h_all[h, :, cols].astype(F32)
        gate_sigmoid = jax.nn.sigmoid(gate_sum)
        hidden[halves[h], cols] = (gate_sum * gate_sigmoid * up_sum).astype(BF)
        gate_grad, up_grad = feed_grads(hidden_grad, gate_sum, up_sum, gate_sigmoid)
        value = product(gate_grad, wgt[cols, :]) + product(up_grad, wut[cols, :])
        if t == 0:
            acc[...] = value
        elif t < TILES - 1:
            acc[...] += value
        else:
            e_part[h] = by_owner(acc[...] + value)
            e_done.append(scatter(e_part.at[h], e_recv.at[h]))
    value = jnp.dot(hidden[...], wd[...], preferred_element_type=F32)
    for h, half in enumerate(halves):
        o_part[:, h] = by_owner(value[half])
    place = row_places(counts, order, n_vis, per, group, rows, (n_slots, rows), 0)
    put = jnp.where(place == lax.broadcasted_iota(jnp.int32, (n_slots, rows), 1), 1.0, 0.0).astype(BF)
    for h in range(HALVES):
        e_done[h]()
        e_all[h, pos] = (total(e_recv.at[h], e_part[h, pos], group, pos) + cot_mine[h].astype(F32)).astype(BF)
        e_done[h] = gather(e_all.at[h, pos], e_all.at[h])
    f_done = []
    for h, half in enumerate(halves):
        e_done[h]()
        ig_out[half] = e_all[h].reshape(hr, dl)
        f_part[h] = product(ig_out[half], wst[...]).astype(BF)
        f_done.append(share(f_part.at[h], f_recv.at[h]))
    o_done = scatter(o_part, o_recv)
    second_out[...] = dot_tn(hid_out[...], ig_out[...])
    for h, half in enumerate(halves):
        f_done[h]()
        act_out[half] = (total(f_recv.at[h], f_part[h], n_vis, vis) * slope[half]).astype(BF)

    slot_act = jnp.dot(put, act_out[...], preferred_element_type=F32).astype(BF)
    slabs[...] = product(slot_act, wft[...]).astype(BF).reshape(n_dev, per, vf)
    across_send, _ = pair_of_sems(slabs.at[pl.ds(0, (n_row - 1) * n_vis * (n_col - 1))])
    direct_view = direct.at[pl.ds(0, n_vis * n_col - 1)]
    direct_send, direct_recv = pair_of_sems(direct_view)
    returned_view = returned.at[pl.ds(0, (n_row - 1) * n_vis)]
    back_send, back_recv = pair_of_sems(returned_view)
    for r in rows_out:
        for c in other_cols:
            spread(
                [(slabs.at[pl.ds((r * n_col + c) * n_vis, n_vis)], (vis, row, c))],
                across.at[r, col], across_send, return_sems.at[r],
            )
    spread(
        [(slabs.at[(row * n_col + c) * n_vis + v], (v, row, c)) for v, _, c in row_mates + mates[:n_vis - 1]],
        direct.at[col * n_vis + vis], direct_send, direct_recv,
    )
    first_out[...] = dot_tn(packed_out[...], act_out[...])
    for r in rows_out:
        across[r, col] = slabs[pl.ds((r * n_col + col) * n_vis, n_vis)]
        wait_for(across.at[0, pl.ds(0, n_col - 1)], return_sems.at[r])
        value = across[r, 0].astype(F32)
        for c in range(1, n_col):
            value = value + across[r, c].astype(F32)
        column_sums[r] = value.astype(BF)
        spread([(column_sums.at[r, v], (v, r, col)) for v in all_vis], returned.at[own], back_send, back_recv)
    o_done()
    o_sum = total(o_recv, o_part[pos], group, pos)
    block_out[...] = jnp.concatenate([o_sum[h] + c_all[h, pos].astype(F32) for h in range(HALVES)], axis=0).astype(BF)
    direct[col * n_vis + vis] = slabs[me]
    wait_for(direct_view, direct_recv)
    for i in range(n_vis):
        value = direct[i].astype(F32)
        for c in range(1, n_col):
            value = value + direct[c * n_vis + i].astype(F32)
        returned[row * n_vis + i] = value.astype(BF)
    wait_for(returned_view, back_recv)
    pieces = []
    for i in range(n_vis):
        value = returned[i].astype(F32)
        for r in range(1, n_row):
            value = value + returned[r * n_vis + i].astype(F32)
        pieces.append(value)
    standardized_input = centred * inverse_scale
    slot_out[...] = norm_gradient_pass(
        jnp.concatenate(pieces, axis=1), standardized_input, inverse_scale, gain_row
    )
    for view, sem in sent:
        wait_for(view, sem)


def store_kernel(*refs):
    sources, targets, sems = refs[:4], refs[4:8], refs[8]
    copies = [pltpu.make_async_copy(a, b, sems.at[i]) for i, (a, b) in enumerate(zip(sources, targets))]
    for copy in copies:
        copy.start()
    for copy in copies:
        copy.wait()


def vis_buffers(n_vis, lead, half_rows, width):
    return [
        pltpu.VMEM(lead + (2, half_rows, width), BF),
        pltpu.VMEM(lead + (half_rows, width), BF),
        pltpu.VMEM(lead + (n_vis // 2, half_rows, width), BF),
        pltpu.VMEM(lead + (2, half_rows, width), BF),
    ]


def on_device(
    sizes,
    images,
    counts,
    block_order,
    projector_norm_gain,
    proj_first,
    proj_bias,
    proj_second,
    gate_weight,
    up_weight,
    down_weight,
    cotangent,
):
    n_vis, n_row, n_col = sizes
    group_size = n_row * n_col
    n_dev = n_vis * group_size
    per_device = images.shape[0]
    local_rows = cotangent.shape[0]
    rows = local_rows * group_size
    vf, units = proj_first.shape
    dl, ffl = gate_weight.shape
    hr = rows // HALVES
    gr = local_rows // HALVES
    by_group = pltpu.VMEM((HALVES, group_size, gr, dl), BF)
    owned_halves = pltpu.VMEM((group_size, HALVES, gr, dl), BF)
    by_device = pltpu.VMEM((n_dev, per_device, vf), BF)
    n_sends = 3 * (1 + HALVES * TILES) + 6 * HALVES + 7
    results = pl.pallas_call(
        functools.partial(chain_kernel, sizes),
        out_shape=(
            pltpu.VMEM((local_rows, dl), BF),
            pltpu.VMEM(images.shape, F32),
            pltpu.VMEM((vf, units), F32),
            pltpu.VMEM((units, dl), F32),
        ),
        in_specs=[HBM] * 11,
        out_specs=(VM,) * 4,
        scratch_shapes=[
            pltpu.SMEM(counts.shape, jnp.int32),
            pltpu.SMEM(block_order.shape, jnp.int32),
            pltpu.VMEM(images.shape, BF),
            pltpu.VMEM(projector_norm_gain.shape, F32),
            pltpu.VMEM(cotangent.shape, BF),
            pltpu.VMEM(proj_bias.shape, F32),
            pltpu.VMEM(proj_first.shape, BF),
            pltpu.VMEM(proj_second.shape, BF),
            pltpu.VMEM(gate_weight.shape, BF),
            pltpu.VMEM(up_weight.shape, BF),
            pltpu.VMEM(down_weight.shape, BF),
            pltpu.VMEM((ffl, dl), BF),
            pltpu.VMEM((ffl, dl), BF),
            pltpu.VMEM((dl, units), BF),
            pltpu.VMEM((units, vf), BF),
            pltpu.VMEM((n_vis, per_device, vf), BF),
            by_device,
            pltpu.VMEM((HALVES, gr, dl), BF),
            owned_halves,
            pltpu.VMEM((rows, dl), BF),
            by_device,
            pltpu.VMEM((n_row, n_col, n_vis, per_device, vf), BF),
            pltpu.VMEM((n_row, n_vis, per_device, vf), BF),
            pltpu.VMEM((n_row * n_vis, per_device, vf), BF),
            pltpu.VMEM((n_col * n_vis, per_device, vf), BF),
            pltpu.VMEM((HALVES, hr, units), BF),
            pltpu.VMEM((HALVES, n_vis, hr, units), BF),
            *vis_buffers(n_vis, (), rows // 2, ffl),
            *vis_buffers(n_vis, (HALVES, TILES), hr // 2, 2 * ffl // TILES),
            pltpu.VMEM((HALVES, hr, units), BF),
            pltpu.VMEM((HALVES, n_vis, hr, units), BF),
            *[by_group] * 6,
            owned_halves,
            owned_halves,
            pltpu.VMEM((rows, vf), BF),
            pltpu.VMEM((rows, units), BF),
            pltpu.VMEM((rows, units), BF),
            pltpu.VMEM((rows, dl), BF),
            pltpu.VMEM((rows, units), F32),
            pltpu.VMEM((rows, dl), BF),
            pltpu.VMEM((hr, dl), F32),
            pltpu.VMEM((rows, ffl), BF),
            pltpu.SemaphoreType.DMA((11,)),
            pltpu.SemaphoreType.DMA((n_row,)),
            pltpu.SemaphoreType.DMA((n_row,)),
            pltpu.SemaphoreType.DMA((2 * n_sends,)),
        ],
        compiler_params=pltpu.CompilerParams(
            collective_id=0, has_side_effects=True, vmem_limit_bytes=48 << 20
        ),
    )(
        *[
            pltpu.with_memory_space_constraint(x, pltpu.HBM)
            for x in (
                counts, block_order, images, projector_norm_gain, cotangent,
                proj_bias, proj_first, proj_second, gate_weight, up_weight, down_weight,
            )
        ]
    )
    return pl.pallas_call(
        store_kernel,
        out_shape=tuple(pltpu.HBM(r.shape, r.dtype) for r in results),
        in_specs=[VM] * 4,
        out_specs=(HBM,) * 4,
        scratch_shapes=[pltpu.SemaphoreType.DMA((4,))],
        compiler_params=pltpu.CompilerParams(vmem_limit_bytes=1 << 20),
    )(*[pltpu.with_memory_space_constraint(r, pltpu.VMEM) for r in results])


def solution(mesh):
    in_specs = (
        P(("vis", "row", "col"), None),
        P(),
        P(),
        P(),
        P("vis", ("row", "col")),
        P(("row", "col")),
        P(("row", "col"), "vis"),
        P("vis", ("row", "col")),
        P("vis", ("row", "col")),
        P(("row", "col"), "vis"),
        P(("row", "col"), "vis"),
    )
    out_specs = (
        P(("row", "col"), "vis"),
        P(("vis", "row", "col"), None),
        P("vis", ("row", "col")),
        P(("row", "col"), "vis"),
    )
    sizes = (mesh.shape["vis"], mesh.shape["row"], mesh.shape["col"])
    return jax.shard_map(
        functools.partial(on_device, sizes), mesh=mesh, in_specs=in_specs, out_specs=out_specs, check_vma=False
    )
```
